128 devices in a mesh: req: 4 (over x), tp: 32 (over z, y, core).
Axes of the slice: x: 4, y: 4, z: 4, core: 2. Of those that a mesh axis runs over, the one named last changes fastest.
Arguments:
- step_inputs: bfloat16 [4, 256, 1536], P(None, ('req', 'tp')), may hold values from -6 to 6
- qkv_weight: bfloat16 [1536, 2048], replicated, may hold values from -0.15625 to 0.15625
- qkv_bias: float32 [2048], replicated, may hold values from -8 to 8
- out_weight: bfloat16 [1536, 1536], P('tp'), may hold values from -0.15625 to 0.15625
- gate_weight: bfloat16 [1536, 8960], P(None, 'tp'), may hold values from -0.15625 to 0.15625
- up_weight: bfloat16 [1536, 8960], P(None, 'tp'), may hold values from -0.15625 to 0.15625
- down_weight: bfloat16 [8960, 1536], P('tp'), may hold values from -0.0625 to 0.0625
- cache_keys: bfloat16 [256, 4096, 256], P(('req', 'tp')), may hold values from -60 to 60
- cache_values: bfloat16 [256, 4096, 256], P(('req', 'tp')), may hold values from -24 to 24
- lengths: int32 [32, 8], replicated, may hold values from 1 to 4096, as said below
- parents: int32 [4, 32, 8], replicated, may hold values from 0 to 7
- slot_request: int32 [32], replicated, may hold values from 0 to 31, each once
Outputs:
- outputs: bfloat16 [4, 256, 1536], P(None, ('req', 'tp'))
The draws below stay inside these ranges and needn't reach their ends.
Inputs may be any that keep to these rules, and one draw needn't show every extreme that they name: lengths[r, c] is the number of cached positions of beam c of request r; some beam has exactly 4096. parents[t, r, b] names a beam of the same request r. `slot_request`: a permutation of the requests; slots 8 * i to 8 * i + 7 are rows of index i of req.
All inputs are finite; a program needn't handle non-finite values.
Results may differ from the reference program's by a relative error of at most 0.022.
The reference program's roundings to bfloat16 on the way count: a program that leaves them out, or rounds other values in their place, can miss the bound.
Values may be sent and summed in bfloat16 or wider, within the bound.
No kernel may reach another device: no remote copies, remote signals or barrier semaphores. Data moves between devices by JAX's collectives and lax.ppermute only.
A program may use at most 128 MiB of HBM per device.

```python
import jax
import jax.numpy as jnp
from jax import lax

D = 1536
Q_HEADS = 12
KV_HEADS = 2
HEAD_DIM = 128
FF = 8960
BEAMS = 8
STEPS = 4
LEN = 4096
REQUESTS = 32
ATTN_WIDTH = 1536
KV_WIDTH = 256
QKV = 2048


def draw_cache_keys(key, part):
    shape = (REQUESTS * BEAMS, LEN, KV_HEADS * HEAD_DIM)
    values = jnp.clip(2.5 * jax.random.normal(key, shape, jnp.float32), -15.0, 15.0)
    return values.astype(jnp.bfloat16)


def draw_qkv_bias(key, part):
    total = (Q_HEADS + 2 * KV_HEADS) * HEAD_DIM
    noise = jax.random.normal(key, (total,), jnp.float32)
    values = 0.5 * noise
    return jnp.clip(values, -8.0, 8.0)


def draw_lengths(key, part):
    values = jax.random.randint(key, (REQUESTS, BEAMS), 1, LEN + 1, dtype=jnp.int32)
    return values.at[0, 0].set(LEN)


def place_ends(drawn, stream_key, smallest, top_value):
    spot = [jax.random.randint(jax.random.fold_in(stream_key, axis), (), 0, length) for axis, length in enumerate(drawn.shape)]
    longest = drawn.shape.index(max(drawn.shape))
    beside = spot[:longest] + [(spot[longest] + 1) % drawn.shape[longest]] + spot[longest + 1:]
    return drawn.at[tuple(spot)].set(smallest).at[tuple(beside)].set(top_value)


def block_scale(stream_key, shape, cuts, least, high):
    def one(position, shards_of):
        steps = jax.random.uniform(jax.random.fold_in(jax.random.fold_in(stream_key, 6), position), (shards_of,), jnp.float32, least / len(cuts), high / len(cuts))
        return jnp.repeat(jnp.exp(steps), shape[position] // shards_of).reshape((-1,) + (1,) * (len(shape) - position - 1))

    gain = one(*cuts[0])
    for cut in cuts[1:]:
        gain = gain * one(*cut)
    return gain


def centred(own_key, extent, scale, bound, split=(), held_as=jnp.bfloat16):
    result = jax.random.normal(own_key, extent, jnp.float32) * scale
    if len(split) > 0:
        result = block_scale(own_key, extent, split, -0.22, 0.18) * result
    return jnp.clip(result, min=-bound, max=bound).astype(held_as)


def setup_inputs(seed: int = 0) -> dict:
    key_list = jax.random.split(jax.random.key(seed), 13)
    return {
        "step_inputs": centred(key_list[0], (STEPS, REQUESTS * BEAMS, D), 1.0, 6.0, ((1, 128),)),
        "qkv_weight": centred(key_list[1], (D, QKV), D ** -0.5, 0.15625),
        "qkv_bias": draw_qkv_bias(jax.random.fold_in(key_list[12], 71), 0),
        "out_weight": centred(key_list[3], (ATTN_WIDTH, D), ATTN_WIDTH ** -0.5, 0.15625, ((0, 32),)),
        "gate_weight": centred(key_list[4], (D, FF), D ** -0.5, 0.15625, ((1, 32),)),
        "up_weight": centred(key_list[5], (D, FF), D ** -0.5, 0.15625, ((1, 32),)),
        "down_weight": centred(key_list[6], (FF, D), FF ** -0.5, 0.0625, ((0, 32),)),
        "cache_keys": draw_cache_keys(jax.random.fold_in(key_list[12], 71), 0),
        "cache_values": centred(key_list[8], (REQUESTS * BEAMS, LEN, KV_WIDTH), 4.0, 24.0, ((0, 128),)),
        "lengths": draw_lengths(jax.random.fold_in(key_list[12], 71), 0),
        "parents": place_ends(jax.random.randint(key_list[10], (STEPS, REQUESTS, BEAMS), 0, BEAMS), jax.random.fold_in(key_list[10], 1), 0, BEAMS - 1).astype(jnp.int32),
        "slot_request": jax.random.permutation(key_list[11], REQUESTS).astype(jnp.int32),
    }


theta_base = 1000000.0
norm_eps = 1e-06
masked_score = -1e+30

def rms_normed(values):
    values = values.astype(jnp.float32)
    factor = lax.rsqrt(lax.optimization_barrier(jnp.mean(values * values, axis=-1, keepdims=True)) + norm_eps)
    return (values * factor).astype(jnp.bfloat16)

def rotate(vectors, positions):
    half = vectors.shape[-1] // 2
    freqs = theta_base ** (-jnp.arange(half, dtype=jnp.float32) * 2.0 / vectors.shape[-1])
    angles = positions.astype(jnp.float32)[:, None] * freqs[None, :]
    cosine = jnp.cos(angles)[:, None, :]
    sine = jnp.sin(angles)[:, None, :]
    values = vectors.astype(jnp.float32)
    first = values[..., :half]
    second = values[..., half:]
    return jnp.concatenate([first * cosine - second * sine, second * cosine + first * sine], axis=-1).astype(jnp.bfloat16)

def rounded(values):
    return lax.optimization_barrier(values.astype(jnp.bfloat16)).astype(jnp.float32)

def reference(step_inputs, qkv_weight, qkv_bias, out_weight, gate_weight, up_weight, down_weight, cache_keys, cache_values, lengths, parents, slot_request):
    attn_width = Q_HEADS * HEAD_DIM
    kv_width = KV_HEADS * HEAD_DIM
    group = Q_HEADS // KV_HEADS
    scale = HEAD_DIM ** (-0.5)
    total_rows = REQUESTS * BEAMS
    roots = jnp.broadcast_to(jnp.arange(BEAMS, dtype=jnp.int32)[None, :], (REQUESTS, BEAMS))
    gen_keys = jnp.zeros((STEPS, total_rows, kv_width), jnp.bfloat16)
    gen_values = jnp.zeros((STEPS, total_rows, kv_width), jnp.bfloat16)
    slot_lengths = lengths[slot_request]
    base_rows = (jnp.arange(REQUESTS, dtype=jnp.int32) * BEAMS)[:, None]
    results = []
    for step in range(STEPS):
        roots = jnp.take_along_axis(roots, parents[step], axis=1)
        slot_parents = parents[step][slot_request]
        reorder = (base_rows + slot_parents).reshape(-1)
        gen_keys = jnp.take(gen_keys, reorder, axis=1)
        gen_values = jnp.take(gen_values, reorder, axis=1)
        inputs = step_inputs[step]
        normed = rms_normed(inputs)
        qkv = (jnp.dot(normed, qkv_weight, preferred_element_type=jnp.float32) + qkv_bias).astype(jnp.bfloat16)
        slot_roots = roots[slot_request]
        prefix_lengths = jnp.take_along_axis(slot_lengths, slot_roots, axis=1)
        positions = (prefix_lengths + step).reshape(-1)
        queries = rotate(qkv[:, :attn_width].reshape(total_rows, Q_HEADS, HEAD_DIM), positions)
        new_keys = rotate(qkv[:, attn_width:attn_width + kv_width].reshape(total_rows, KV_HEADS, HEAD_DIM), positions)
        gen_keys = gen_keys.at[step].set(new_keys.reshape(total_rows, kv_width))
        gen_values = gen_values.at[step].set(qkv[:, attn_width + kv_width:])
        cache_rows = slot_request[:, None] * BEAMS + slot_roots
        query_blocks = queries.reshape(REQUESTS, BEAMS, KV_HEADS, group, HEAD_DIM)
        past_keys_all = gen_keys[:step + 1].reshape(step + 1, REQUESTS, BEAMS, KV_HEADS, HEAD_DIM).transpose(1, 0, 2, 3, 4)
        past_values_all = gen_values[:step + 1].reshape(step + 1, REQUESTS, BEAMS, KV_HEADS, HEAD_DIM).transpose(1, 0, 2, 3, 4)

        def one_request(items):
            rows, limits, query_block, past_keys, past_values = items
            keys = jnp.take(cache_keys, rows, axis=0).astype(jnp.float32).reshape(BEAMS, LEN, KV_HEADS, HEAD_DIM)
            values = jnp.take(cache_values, rows, axis=0).astype(jnp.float32).reshape(BEAMS, LEN, KV_HEADS, HEAD_DIM)
            query_block = query_block.astype(jnp.float32)
            prefix_scores = jnp.einsum('bkgd,bpkd->bkgp', query_block, keys) * scale
            live = (jnp.arange(LEN, dtype=jnp.int32)[None, :] < limits[:, None])[:, None, None, :]
            prefix_scores = jnp.where(live, prefix_scores, masked_score)
            recent_scores = jnp.einsum('bkgd,sbkd->bkgs', query_block, past_keys.astype(jnp.float32)) * scale
            top = jnp.maximum(lax.optimization_barrier(jnp.max(prefix_scores, axis=-1)), lax.optimization_barrier(jnp.max(recent_scores, axis=-1)))
            prefix_weights = jnp.where(live, jnp.exp(prefix_scores - top[..., None]), 0.0)
            recent_weights = jnp.exp(recent_scores - top[..., None])
            denominator = lax.optimization_barrier(jnp.sum(prefix_weights, axis=-1)) + lax.optimization_barrier(jnp.sum(recent_weights, axis=-1))
            numerator = jnp.einsum('bkgp,bpkd->bkgd', rounded(prefix_weights), values)
            numerator = numerator + jnp.einsum('bkgs,sbkd->bkgd', rounded(recent_weights), past_values.astype(jnp.float32))
            return (numerator / denominator[..., None]).astype(jnp.bfloat16)
        attention = lax.map(one_request, (cache_rows, prefix_lengths, query_blocks, past_keys_all, past_values_all))
        attention = attention.reshape(total_rows, attn_width)
        middle = inputs.astype(jnp.float32) + jnp.dot(attention, out_weight, preferred_element_type=jnp.float32)
        mixed_in = rms_normed(middle)
        gate = jnp.dot(mixed_in, gate_weight, preferred_element_type=jnp.float32)
        upward = jnp.dot(mixed_in, up_weight, preferred_element_type=jnp.float32)
        hidden = (jax.nn.silu(gate) * upward).astype(jnp.bfloat16)
        results.append((middle + jnp.dot(hidden, down_weight, preferred_element_type=jnp.float32)).astype(jnp.bfloat16))
    return jnp.stack(results)
```

```python
import jax
import jax.numpy as jnp
from jax import lax
from jax.sharding import Mesh
from jax.sharding import PartitionSpec as P

Q_HEADS = 12
KV_HEADS = 2

theta_base = 1000000.0
norm_eps = 1e-06
masked_score = -1e30

ALL = ("req", "tpo", "tpi")
TP = ("tpo", "tpi")


def rms_normed(values):
    values = values.astype(jnp.float32)
    factor = lax.rsqrt(jnp.mean(values * values, axis=-1, keepdims=True) + norm_eps)
    return (values * factor).astype(jnp.bfloat16)


def rotate(vectors, positions):
    half = vectors.shape[-1] // 2
    freqs = theta_base ** (-jnp.arange(half, dtype=jnp.float32) * 2.0 / vectors.shape[-1])
    angles = positions.astype(jnp.float32)[..., None] * freqs
    cosine = jnp.cos(angles)[..., None, :]
    sine = jnp.sin(angles)[..., None, :]
    values = vectors.astype(jnp.float32)
    first = values[..., :half]
    second = values[..., half:]
    return jnp.concatenate(
        [first * cosine - second * sine, second * cosine + first * sine], axis=-1
    ).astype(jnp.bfloat16)


def per_device(
    step_inputs,
    qkv_weight,
    qkv_bias,
    out_weight,
    gate_weight,
    up_weight,
    down_weight,
    cache_keys,
    cache_values,
    lengths,
    parents,
    slot_request,
):
    steps, rows_dev, width = step_inputs.shape
    beams = parents.shape[2]
    requests = slot_request.shape[0]
    n_req = lax.axis_size("req")
    n_o = lax.axis_size("tpo")
    n_i = lax.axis_size("tpi")
    tp_count = n_o * n_i
    group_requests = requests // n_req
    group_rows = group_requests * beams
    owned, context, kv_width = cache_keys.shape
    head_dim = kv_width // KV_HEADS
    group = Q_HEADS // KV_HEADS
    attn_width = Q_HEADS * head_dim
    scale = head_dim ** (-0.5)
    assert owned * n_i == beams

    req_index = lax.axis_index("req")
    tp_index = lax.axis_index("tpo") * n_i + lax.axis_index("tpi")
    j = lax.axis_index("tpi")
    flat = req_index * tp_count + tp_index
    r = flat // n_i

    inverse = (
        jnp.zeros((requests,), jnp.int32)
        .at[slot_request]
        .set(jnp.arange(requests, dtype=jnp.int32))
    )

    x_all = lax.all_gather(jnp.swapaxes(step_inputs, 0, 1), ALL, axis=0, tiled=True)

    x_req = lax.dynamic_slice_in_dim(x_all, inverse[r] * beams, beams, 0)
    normed = rms_normed(x_req)
    qkv = (
        jnp.dot(normed, qkv_weight, preferred_element_type=jnp.float32) + qkv_bias
    ).astype(jnp.bfloat16)

    par = parents[:, r, :]
    root = jnp.arange(beams, dtype=jnp.int32)
    roots = []
    for t in range(steps):
        root = root[par[t]]
        roots.append(root)
    roots = jnp.stack(roots, axis=1)
    len_r = lengths[r]
    positions = len_r[roots] + jnp.arange(steps, dtype=jnp.int32)[None, :]

    queries = rotate(qkv[..., :attn_width].reshape(beams, steps, Q_HEADS, head_dim), positions)
    new_keys = rotate(
        qkv[..., attn_width : attn_width + kv_width].reshape(beams, steps, KV_HEADS, head_dim),
        positions,
    )
    new_values = qkv[..., attn_width + kv_width :].reshape(beams, steps, KV_HEADS, head_dim)

    keys = cache_keys.reshape(owned, context, KV_HEADS, head_dim)
    values = cache_values.reshape(owned, context, KV_HEADS, head_dim)
    qg = queries.reshape(beams, steps, KV_HEADS, group, head_dim)
    scores = jnp.einsum(
        "btkgd,cpkd->cbtkgp", qg, keys, preferred_element_type=jnp.float32
    ) * scale
    my_beams = j * owned + jnp.arange(owned, dtype=jnp.int32)
    limits = len_r[my_beams]
    live = (jnp.arange(context, dtype=jnp.int32)[None, :] < limits[:, None])[
        :, None, None, None, None, :
    ]
    scores = jnp.where(live, scores, masked_score)
    peak = jnp.max(scores, axis=-1)
    weights = jnp.where(live, jnp.exp(scores - peak[..., None]), 0.0)
    total = jnp.sum(weights, axis=-1)
    output = jnp.einsum(
        "cbtkgp,cpkd->cbtkgd",
        weights.astype(jnp.bfloat16),
        values,
        preferred_element_type=jnp.float32,
    )
    chosen = (roots[None, :, :] == my_beams[:, None, None])[..., None, None]
    peak = jnp.sum(jnp.where(chosen, peak, 0.0), axis=0)
    total = jnp.sum(jnp.where(chosen, total, 0.0), axis=0)
    output = jnp.sum(jnp.where(chosen[..., None], output, 0.0), axis=0)
    packed = jnp.concatenate([output, peak[..., None], total[..., None]], axis=-1)
    packed = packed.reshape(n_i, owned, steps, KV_HEADS, group, head_dim + 2)
    packed = lax.psum_scatter(packed, "tpi", scatter_dimension=0, tiled=True)[0]
    part_output = packed[..., :head_dim]
    part_peak = packed[..., head_dim]
    part_total = packed[..., head_dim + 1]

    anc = []
    for t in range(steps):
        cur = jnp.arange(beams, dtype=jnp.int32)
        row = [None] * steps
        row[t] = cur
        for step in range(t, 0, -1):
            cur = par[step][cur]
            row[step - 1] = cur
        for u in range(t + 1, steps):
            row[u] = jnp.arange(beams, dtype=jnp.int32)
        anc.append(jnp.stack(row, axis=0))
    anc = jnp.stack(anc, axis=0)
    anc_mine = lax.dynamic_slice_in_dim(anc, j * owned, owned, 2)
    anc_mine = jnp.transpose(anc_mine, (2, 0, 1))
    u_index = jnp.broadcast_to(jnp.arange(steps, dtype=jnp.int32), anc_mine.shape)
    hist_keys = new_keys[anc_mine, u_index]
    hist_values = new_values[anc_mine, u_index]
    q_mine = lax.dynamic_slice_in_dim(qg, j * owned, owned, 0)
    recent_scores = jnp.einsum(
        "ctkgd,ctukd->ctkgu", q_mine, hist_keys, preferred_element_type=jnp.float32
    ) * scale
    causal = (
        jnp.arange(steps, dtype=jnp.int32)[None, :] <= jnp.arange(steps, dtype=jnp.int32)[:, None]
    )[None, :, None, None, :]
    recent_scores = jnp.where(causal, recent_scores, masked_score)
    top = jnp.maximum(part_peak, jnp.max(recent_scores, axis=-1))
    factor = jnp.exp(part_peak - top)
    recent_weights = jnp.where(causal, jnp.exp(recent_scores - top[..., None]), 0.0)
    denominator = part_total * factor + jnp.sum(recent_weights, axis=-1)
    numerator = part_output * factor[..., None] + jnp.einsum(
        "ctkgu,ctukd->ctkgd",
        recent_weights.astype(jnp.bfloat16),
        hist_values,
        preferred_element_type=jnp.float32,
    )
    attention = (
        (numerator / denominator[..., None]).reshape(owned, steps, attn_width).astype(jnp.bfloat16)
    )

    att_all = lax.all_gather(attention, ALL, axis=0, tiled=True)
    my_requests = lax.dynamic_slice_in_dim(slot_request, req_index * group_requests, group_requests)
    att_group = att_all.reshape(requests, beams, steps, attn_width)[my_requests].reshape(
        group_rows, steps, attn_width
    )
    x_group = lax.dynamic_slice_in_dim(x_all, req_index * group_rows, group_rows, 0)

    full_out = lax.all_gather(out_weight, TP, axis=0, tiled=True)
    middle = x_group.astype(jnp.float32) + jnp.dot(
        att_group, full_out, preferred_element_type=jnp.float32
    )
    mixed_in = rms_normed(middle)
    gate = jnp.dot(mixed_in, gate_weight, preferred_element_type=jnp.float32)
    upward = jnp.dot(mixed_in, up_weight, preferred_element_type=jnp.float32)
    hidden = (jax.nn.silu(gate) * upward).astype(jnp.bfloat16)
    lowered = lax.psum_scatter(
        jnp.dot(hidden, down_weight, preferred_element_type=jnp.float32).astype(jnp.bfloat16),
        TP,
        scatter_dimension=0,
        tiled=True,
    ).astype(jnp.float32)
    middle_mine = lax.dynamic_slice_in_dim(middle, tp_index * rows_dev, rows_dev, 0)
    result = (middle_mine + lowered).astype(jnp.bfloat16)
    return jnp.swapaxes(result, 0, 1)


def solution(mesh):
    n_req = mesh.shape["req"]
    n_tp = mesh.shape["tp"]
    inner = 4
    devices = mesh.devices.reshape(n_req, n_tp // inner, inner)
    sub = Mesh(devices, ALL)
    rows = P(None, ALL, None)
    in_specs = (
        rows,
        P(),
        P(),
        P(TP, None),
        P(None, TP),
        P(None, TP),
        P(TP, None),
        P(ALL, None, None),
        P(ALL, None, None),
        P(),
        P(),
        P(),
    )
    return jax.shard_map(per_device, mesh=sub, in_specs=in_specs, out_specs=rows, check_vma=False)
```

```python
import jax
import jax.numpy as jnp
from jax import lax
from jax.sharding import Mesh
from jax.sharding import PartitionSpec as P

Q_HEADS = 12
KV_HEADS = 2

theta_base = 1000000.0
norm_eps = 1e-06
masked_score = -1e30

ALL = ("req", "tpo", "tpi")
TP = ("tpo", "tpi")


def rms_normed(values):
    values = values.astype(jnp.float32)
    factor = lax.rsqrt(jnp.mean(values * values, axis=-1, keepdims=True) + norm_eps)
    return (values * factor).astype(jnp.bfloat16)


def rotate(vectors, positions):
    half = vectors.shape[-1] // 2
    freqs = theta_base ** (-jnp.arange(half, dtype=jnp.float32) * 2.0 / vectors.shape[-1])
    angles = positions.astype(jnp.float32)[..., None] * freqs
    cosine = jnp.cos(angles)[..., None, :]
    sine = jnp.sin(angles)[..., None, :]
    values = vectors.astype(jnp.float32)
    first = values[..., :half]
    second = values[..., half:]
    return jnp.concatenate(
        [first * cosine - second * sine, second * cosine + first * sine], axis=-1
    ).astype(jnp.bfloat16)


def per_device(
    step_inputs,
    qkv_weight,
    qkv_bias,
    out_weight,
    gate_weight,
    up_weight,
    down_weight,
    cache_keys,
    cache_values,
    lengths,
    parents,
    slot_request,
):
    steps, rows_dev, width = step_inputs.shape
    beams = parents.shape[2]
    requests = slot_request.shape[0]
    n_req = lax.axis_size("req")
    n_o = lax.axis_size("tpo")
    n_i = lax.axis_size("tpi")
    tp_count = n_o * n_i
    group_requests = requests // n_req
    group_rows = group_requests * beams
    owned, context, kv_width = cache_keys.shape
    head_dim = kv_width // KV_HEADS
    group = Q_HEADS // KV_HEADS
    attn_width = Q_HEADS * head_dim
    scale = head_dim ** (-0.5)
    assert owned * n_i == beams

    req_index = lax.axis_index("req")
    tp_index = lax.axis_index("tpo") * n_i + lax.axis_index("tpi")
    j = lax.axis_index("tpi")
    flat = req_index * tp_count + tp_index
    r = flat // n_i

    inverse = (
        jnp.zeros((requests,), jnp.int32)
        .at[slot_request]
        .set(jnp.arange(requests, dtype=jnp.int32))
    )

    x_plane = lax.all_gather(jnp.swapaxes(step_inputs, 0, 1), ("req", "tpo"), axis=0, tiled=False)
    my_slots = lax.dynamic_slice_in_dim(x_plane, req_index * group_requests, group_requests, 0)
    carry = jnp.concatenate([x_plane[inverse[r]][None], my_slots], axis=0)
    carry = lax.all_gather(carry, "tpi", axis=0, tiled=False)
    x_req = carry[:, 0].reshape(beams, steps, width)
    x_group = jnp.swapaxes(carry[:, 1:], 0, 1).reshape(group_rows, steps, width)

    normed = rms_normed(x_req)
    qkv = (
        jnp.dot(normed, qkv_weight, preferred_element_type=jnp.float32) + qkv_bias
    ).astype(jnp.bfloat16)

    par = parents[:, r, :]
    root = jnp.arange(beams, dtype=jnp.int32)
    roots = []
    for t in range(steps):
        root = root[par[t]]
        roots.append(root)
    roots = jnp.stack(roots, axis=1)
    len_r = lengths[r]
    positions = len_r[roots] + jnp.arange(steps, dtype=jnp.int32)[None, :]

    queries = rotate(qkv[..., :attn_width].reshape(beams, steps, Q_HEADS, head_dim), positions)
    new_keys = rotate(
        qkv[..., attn_width : attn_width + kv_width].reshape(beams, steps, KV_HEADS, head_dim),
        positions,
    )
    new_values = qkv[..., attn_width + kv_width :].reshape(beams, steps, KV_HEADS, head_dim)

    qg = queries.reshape(beams, steps, KV_HEADS, group, head_dim)
    score_parts = []
    for k in range(KV_HEADS):
        keys_k = cache_keys[:, :, k * head_dim : (k + 1) * head_dim]
        score_parts.append(
            jnp.einsum("btgd,cpd->cbtgp", qg[:, :, k], keys_k, preferred_element_type=jnp.float32)
        )
    scores = jnp.stack(score_parts, axis=3) * scale
    my_beams = j * owned + jnp.arange(owned, dtype=jnp.int32)
    limits = len_r[my_beams]
    live = (jnp.arange(context, dtype=jnp.int32)[None, :] < limits[:, None])[
        :, None, None, None, None, :
    ]
    scores = jnp.where(live, scores, masked_score)
    peak = jnp.max(scores, axis=-1)
    weights = jnp.where(live, jnp.exp(scores - peak[..., None]), 0.0)
    total = jnp.sum(weights, axis=-1)
    weights = weights.astype(jnp.bfloat16)
    output = jnp.stack(
        [
            jnp.einsum(
                "cbtgp,cpd->cbtgd",
                weights[:, :, :, k],
                cache_values[:, :, k * head_dim : (k + 1) * head_dim],
                preferred_element_type=jnp.float32,
            )
            for k in range(KV_HEADS)
        ],
        axis=3,
    )
    chosen = (roots[None, :, :] == my_beams[:, None, None])[..., None, None]
    peak = jnp.sum(jnp.where(chosen, peak, 0.0), axis=0)
    total = jnp.sum(jnp.where(chosen, total, 0.0), axis=0)
    output = jnp.sum(jnp.where(chosen[..., None], output, 0.0), axis=0)
    packed = jnp.concatenate([output, peak[..., None], total[..., None]], axis=-1)
    packed = packed.reshape(n_i, owned, steps, KV_HEADS, group, head_dim + 2)
    packed = lax.psum_scatter(packed, "tpi", scatter_dimension=0, tiled=True)[0]
    part_output = packed[..., :head_dim]
    part_peak = packed[..., head_dim]
    part_total = packed[..., head_dim + 1]

    anc = []
    for t in range(steps):
        cur = jnp.arange(beams, dtype=jnp.int32)
        row = [None] * steps
        row[t] = cur
        for step in range(t, 0, -1):
            cur = par[step][cur]
            row[step - 1] = cur
        for u in range(t + 1, steps):
            row[u] = jnp.arange(beams, dtype=jnp.int32)
        anc.append(jnp.stack(row, axis=0))
    anc = jnp.stack(anc, axis=0)
    anc_mine = lax.dynamic_slice_in_dim(anc, j * owned, owned, 2)
    anc_mine = jnp.transpose(anc_mine, (2, 0, 1))
    u_index = jnp.broadcast_to(jnp.arange(steps, dtype=jnp.int32), anc_mine.shape)
    hist_keys = new_keys[anc_mine, u_index]
    hist_values = new_values[anc_mine, u_index]
    q_mine = lax.dynamic_slice_in_dim(qg, j * owned, owned, 0)
    recent_scores = jnp.einsum(
        "ctkgd,ctukd->ctkgu", q_mine, hist_keys, preferred_element_type=jnp.float32
    ) * scale
    causal = (
        jnp.arange(steps, dtype=jnp.int32)[None, :] <= jnp.arange(steps, dtype=jnp.int32)[:, None]
    )[None, :, None, None, :]
    recent_scores = jnp.where(causal, recent_scores, masked_score)
    top = jnp.maximum(part_peak, jnp.max(recent_scores, axis=-1))
    factor = jnp.exp(part_peak - top)
    recent_weights = jnp.where(causal, jnp.exp(recent_scores - top[..., None]), 0.0)
    denominator = part_total * factor + jnp.sum(recent_weights, axis=-1)
    numerator = part_output * factor[..., None] + jnp.einsum(
        "ctkgu,ctukd->ctkgd",
        recent_weights.astype(jnp.bfloat16),
        hist_values,
        preferred_element_type=jnp.float32,
    )
    attention = (
        (numerator / denominator[..., None]).reshape(owned, steps, attn_width).astype(jnp.bfloat16)
    )

    att_plane = lax.all_gather(attention, ("req", "tpo"), axis=0, tiled=False)
    my_requests = lax.dynamic_slice_in_dim(slot_request, req_index * group_requests, group_requests)
    att_mine = att_plane[my_requests]
    att_group = lax.all_gather(att_mine, "tpi", axis=0, tiled=False)
    att_group = jnp.swapaxes(att_group, 0, 1).reshape(group_rows, steps, attn_width)

    full_out = lax.all_gather(out_weight, TP, axis=0, tiled=True)
    middle = x_group.astype(jnp.float32) + jnp.dot(
        att_group, full_out, preferred_element_type=jnp.float32
    )
    mixed_in = rms_normed(middle)
    gate = jnp.dot(mixed_in, gate_weight, preferred_element_type=jnp.float32)
    upward = jnp.dot(mixed_in, up_weight, preferred_element_type=jnp.float32)
    hidden = (jax.nn.silu(gate) * upward).astype(jnp.bfloat16)
    partial = jnp.dot(hidden, down_weight, preferred_element_type=jnp.float32)
    partial = partial.reshape(tp_count, rows_dev * steps, width)
    lowered = lax.psum_scatter(partial, TP, scatter_dimension=0, tiled=True)
    lowered = lowered.reshape(rows_dev, steps, width)
    middle_mine = lax.dynamic_slice_in_dim(middle, tp_index * rows_dev, rows_dev, 0)
    result = (middle_mine + lowered).astype(jnp.bfloat16)
    return jnp.swapaxes(result, 0, 1)


def solution(mesh):
    n_req = mesh.shape["req"]
    n_tp = mesh.shape["tp"]
    inner = 4
    devices = mesh.devices.reshape(n_req, n_tp // inner, inner)
    sub = Mesh(devices, ALL)
    rows = P(None, ALL, None)
    in_specs = (
        rows,
        P(),
        P(),
        P(TP, None),
        P(None, TP),
        P(None, TP),
        P(TP, None),
        P(ALL, None, None),
        P(ALL, None, None),
        P(),
        P(),
        P(),
    )
    return jax.shard_map(per_device, mesh=sub, in_specs=in_specs, out_specs=rows, check_vma=False)
```

```python
import jax
import jax.numpy as jnp
from jax import lax
from jax.sharding import Mesh
from jax.sharding import PartitionSpec as P

Q_HEADS = 12
KV_HEADS = 2

theta_base = 1000000.0
norm_eps = 1e-06
masked_score = -1e30

ALL = ("req", "tpo", "tpi")
TP = ("tpo", "tpi")


def rms_normed(values):
    values = values.astype(jnp.float32)
    factor = lax.rsqrt(jnp.mean(values * values, axis=-1, keepdims=True) + norm_eps)
    return (values * factor).astype(jnp.bfloat16)


def rotate(vectors, positions):
    half = vectors.shape[-1] // 2
    freqs = theta_base ** (-jnp.arange(half, dtype=jnp.float32) * 2.0 / vectors.shape[-1])
    angles = positions.astype(jnp.float32)[..., None] * freqs
    cosine = jnp.cos(angles)[..., None, :]
    sine = jnp.sin(angles)[..., None, :]
    values = vectors.astype(jnp.float32)
    first = values[..., :half]
    second = values[..., half:]
    return jnp.concatenate(
        [first * cosine - second * sine, second * cosine + first * sine], axis=-1
    ).astype(jnp.bfloat16)


def per_device(
    step_inputs,
    qkv_weight,
    qkv_bias,
    out_weight,
    gate_weight,
    up_weight,
    down_weight,
    cache_keys,
    cache_values,
    lengths,
    parents,
    slot_request,
):
    steps, rows_dev, width = step_inputs.shape
    beams = parents.shape[2]
    requests = slot_request.shape[0]
    n_req = lax.axis_size("req")
    n_o = lax.axis_size("tpo")
    n_i = lax.axis_size("tpi")
    tp_count = n_o * n_i
    group_requests = requests // n_req
    group_rows = group_requests * beams
    owned, context, kv_width = cache_keys.shape
    head_dim = kv_width // KV_HEADS
    group = Q_HEADS // KV_HEADS
    attn_width = Q_HEADS * head_dim
    scale = head_dim ** (-0.5)
    assert owned * n_i == beams

    req_index = lax.axis_index("req")
    tp_index = lax.axis_index("tpo") * n_i + lax.axis_index("tpi")
    j = lax.axis_index("tpi")
    flat = req_index * tp_count + tp_index
    r = flat // n_i

    inverse = (
        jnp.zeros((requests,), jnp.int32)
        .at[slot_request]
        .set(jnp.arange(requests, dtype=jnp.int32))
    )

    x_all = lax.all_gather(jnp.swapaxes(step_inputs, 0, 1), ALL, axis=0, tiled=True)
    x_req = lax.dynamic_slice_in_dim(x_all, inverse[r] * beams, beams, 0)
    x_group = lax.dynamic_slice_in_dim(x_all, req_index * group_rows, group_rows, 0)

    normed = rms_normed(x_req)
    qkv = (
        jnp.dot(normed, qkv_weight, preferred_element_type=jnp.float32) + qkv_bias
    ).astype(jnp.bfloat16)

    par = parents[:, r, :]
    root = jnp.arange(beams, dtype=jnp.int32)
    roots = []
    for t in range(steps):
        root = root[par[t]]
        roots.append(root)
    roots = jnp.stack(roots, axis=1)
    len_r = lengths[r]
    positions = len_r[roots] + jnp.arange(steps, dtype=jnp.int32)[None, :]

    queries = rotate(qkv[..., :attn_width].reshape(beams, steps, Q_HEADS, head_dim), positions)
    new_keys = rotate(
        qkv[..., attn_width : attn_width + kv_width].reshape(beams, steps, KV_HEADS, head_dim),
        positions,
    )
    new_values = qkv[..., attn_width + kv_width :].reshape(beams, steps, KV_HEADS, head_dim)

    qg = queries.reshape(beams, steps, KV_HEADS, group, head_dim)
    score_parts = []
    for k in range(KV_HEADS):
        keys_k = cache_keys[:, :, k * head_dim : (k + 1) * head_dim]
        score_parts.append(
            jnp.einsum("btgd,cpd->cbtgp", qg[:, :, k], keys_k, preferred_element_type=jnp.float32)
        )
    scores = jnp.stack(score_parts, axis=3) * scale
    my_beams = j * owned + jnp.arange(owned, dtype=jnp.int32)
    limits = len_r[my_beams]
    live = (jnp.arange(context, dtype=jnp.int32)[None, :] < limits[:, None])[
        :, None, None, None, None, :
    ]
    scores = jnp.where(live, scores, masked_score)
    peak = jnp.max(scores, axis=-1)
    weights = jnp.where(live, jnp.exp(scores - peak[..., None]), 0.0)
    total = jnp.sum(weights, axis=-1)
    weights = weights.astype(jnp.bfloat16)
    output = jnp.stack(
        [
            jnp.einsum(
                "cbtgp,cpd->cbtgd",
                weights[:, :, :, k],
                cache_values[:, :, k * head_dim : (k + 1) * head_dim],
                preferred_element_type=jnp.float32,
            )
            for k in range(KV_HEADS)
        ],
        axis=3,
    )
    chosen = (roots[None, :, :] == my_beams[:, None, None])[..., None, None]
    peak = jnp.sum(jnp.where(chosen, peak, 0.0), axis=0)
    total = jnp.sum(jnp.where(chosen, total, 0.0), axis=0)
    output = jnp.sum(jnp.where(chosen[..., None], output, 0.0), axis=0)
    packed = jnp.concatenate([output, peak[..., None], total[..., None]], axis=-1)
    packed = packed.reshape(n_i, owned, steps, KV_HEADS, group, head_dim + 2)
    packed = lax.psum_scatter(packed, "tpi", scatter_dimension=0, tiled=True)[0]
    part_output = packed[..., :head_dim]
    part_peak = packed[..., head_dim]
    part_total = packed[..., head_dim + 1]

    anc = []
    for t in range(steps):
        cur = jnp.arange(beams, dtype=jnp.int32)
        row = [None] * steps
        row[t] = cur
        for step in range(t, 0, -1):
            cur = par[step][cur]
            row[step - 1] = cur
        for u in range(t + 1, steps):
            row[u] = jnp.arange(beams, dtype=jnp.int32)
        anc.append(jnp.stack(row, axis=0))
    anc = jnp.stack(anc, axis=0)
    anc_mine = lax.dynamic_slice_in_dim(anc, j * owned, owned, 2)
    anc_mine = jnp.transpose(anc_mine, (2, 0, 1))
    u_index = jnp.broadcast_to(jnp.arange(steps, dtype=jnp.int32), anc_mine.shape)
    hist_keys = new_keys[anc_mine, u_index]
    hist_values = new_values[anc_mine, u_index]
    q_mine = lax.dynamic_slice_in_dim(qg, j * owned, owned, 0)
    recent_scores = jnp.einsum(
        "ctkgd,ctukd->ctkgu", q_mine, hist_keys, preferred_element_type=jnp.float32
    ) * scale
    causal = (
        jnp.arange(steps, dtype=jnp.int32)[None, :] <= jnp.arange(steps, dtype=jnp.int32)[:, None]
    )[None, :, None, None, :]
    recent_scores = jnp.where(causal, recent_scores, masked_score)
    top = jnp.maximum(part_peak, jnp.max(recent_scores, axis=-1))
    factor = jnp.exp(part_peak - top)
    recent_weights = jnp.where(causal, jnp.exp(recent_scores - top[..., None]), 0.0)
    denominator = part_total * factor + jnp.sum(recent_weights, axis=-1)
    numerator = part_output * factor[..., None] + jnp.einsum(
        "ctkgu,ctukd->ctkgd",
        recent_weights.astype(jnp.bfloat16),
        hist_values,
        preferred_element_type=jnp.float32,
    )
    attention = (
        (numerator / denominator[..., None]).reshape(owned, steps, attn_width).astype(jnp.bfloat16)
    )

    att_all = lax.all_gather(attention, ALL, axis=0, tiled=True)
    my_requests = lax.dynamic_slice_in_dim(slot_request, req_index * group_requests, group_requests)
    att_group = att_all.reshape(requests, beams, steps, attn_width)[my_requests].reshape(
        group_rows, steps, attn_width
    )

    full_out = lax.all_gather(out_weight, TP, axis=0, tiled=True)
    middle = x_group.astype(jnp.float32) + jnp.dot(
        att_group, full_out, preferred_element_type=jnp.float32
    )
    mixed_in = rms_normed(middle)
    gate = jnp.dot(mixed_in, gate_weight, preferred_element_type=jnp.float32)
    upward = jnp.dot(mixed_in, up_weight, preferred_element_type=jnp.float32)
    hidden = (jax.nn.silu(gate) * upward).astype(jnp.bfloat16)
    partial = jnp.dot(hidden, down_weight, preferred_element_type=jnp.float32).astype(jnp.bfloat16)
    chunk = rows_dev * steps * width
    partial = partial.reshape(tp_count, 16, chunk // 16)
    lowered = lax.psum_scatter(partial, TP, scatter_dimension=0, tiled=True)
    lowered = lowered.reshape(rows_dev, steps, width).astype(jnp.float32)
    middle_mine = lax.dynamic_slice_in_dim(middle, tp_index * rows_dev, rows_dev, 0)
    result = (middle_mine + lowered).astype(jnp.bfloat16)
    return jnp.swapaxes(result, 0, 1)


def solution(mesh):
    n_req = mesh.shape["req"]
    n_tp = mesh.shape["tp"]
    inner = 4
    devices = mesh.devices.reshape(n_req, n_tp // inner, inner)
    sub = Mesh(devices, ALL)
    rows = P(None, ALL, None)
    in_specs = (
        rows,
        P(),
        P(),
        P(TP, None),
        P(None, TP),
        P(None, TP),
        P(TP, None),
        P(ALL, None, None),
        P(ALL, None, None),
        P(),
        P(),
        P(),
    )
    return jax.shard_map(per_device, mesh=sub, in_specs=in_specs, out_specs=rows, check_vma=False)
```

```python
import jax
import jax.numpy as jnp
from jax import lax
from jax.sharding import Mesh
from jax.sharding import PartitionSpec as P

Q_HEADS = 12
KV_HEADS = 2

theta_base = 1000000.0
norm_eps = 1e-06
masked_score = -1e30

ALL = ("req", "tpo", "tpi")
TP = ("tpo", "tpi")


def rms_normed(values):
    values = values.astype(jnp.float32)
    factor = lax.rsqrt(jnp.mean(values * values, axis=-1, keepdims=True) + norm_eps)
    return (values * factor).astype(jnp.bfloat16)


def rotate(vectors, positions):
    half = vectors.shape[-1] // 2
    freqs = theta_base ** (-jnp.arange(half, dtype=jnp.float32) * 2.0 / vectors.shape[-1])
    angles = positions.astype(jnp.float32)[..., None] * freqs
    cosine = jnp.cos(angles)[..., None, :]
    sine = jnp.sin(angles)[..., None, :]
    values = vectors.astype(jnp.float32)
    first = values[..., :half]
    second = values[..., half:]
    return jnp.concatenate(
        [first * cosine - second * sine, second * cosine + first * sine], axis=-1
    ).astype(jnp.bfloat16)


def per_device(
    step_inputs,
    qkv_weight,
    qkv_bias,
    out_weight,
    gate_weight,
    up_weight,
    down_weight,
    cache_keys,
    cache_values,
    lengths,
    parents,
    slot_request,
):
    steps, rows_dev, width = step_inputs.shape
    beams = parents.shape[2]
    requests = slot_request.shape[0]
    n_req = lax.axis_size("req")
    n_o = lax.axis_size("tpo")
    n_i = lax.axis_size("tpi")
    tp_count = n_o * n_i
    group_requests = requests // n_req
    group_rows = group_requests * beams
    owned, context, kv_width = cache_keys.shape
    head_dim = kv_width // KV_HEADS
    group = Q_HEADS // KV_HEADS
    attn_width = Q_HEADS * head_dim
    scale = head_dim ** (-0.5)
    assert owned * n_i == beams

    req_index = lax.axis_index("req")
    tp_index = lax.axis_index("tpo") * n_i + lax.axis_index("tpi")
    j = lax.axis_index("tpi")
    flat = req_index * tp_count + tp_index
    r = flat // n_i

    inverse = (
        jnp.zeros((requests,), jnp.int32)
        .at[slot_request]
        .set(jnp.arange(requests, dtype=jnp.int32))
    )

    column_rows = out_weight.shape[0]
    share = column_rows // n_req
    w_share = lax.dynamic_slice_in_dim(out_weight, req_index * share, share, 0)
    carry = jnp.concatenate(
        [jnp.swapaxes(step_inputs, 0, 1).reshape(rows_dev * steps, width), w_share], axis=0
    )
    carry = lax.all_gather(carry, ALL, axis=0, tiled=False)
    x_all = carry[:, : rows_dev * steps].reshape(requests * beams, steps, width)
    full_out = (
        carry[:, rows_dev * steps :]
        .reshape(n_req, tp_count, share, width)
        .transpose(1, 0, 2, 3)
        .reshape(tp_count * column_rows, width)
    )
    x_req = lax.dynamic_slice_in_dim(x_all, inverse[r] * beams, beams, 0)
    x_group = lax.dynamic_slice_in_dim(x_all, req_index * group_rows, group_rows, 0)

    normed = rms_normed(x_req)
    qkv = (
        jnp.dot(normed, qkv_weight, preferred_element_type=jnp.float32) + qkv_bias
    ).astype(jnp.bfloat16)

    par = parents[:, r, :]
    root = jnp.arange(beams, dtype=jnp.int32)
    roots = []
    for t in range(steps):
        root = root[par[t]]
        roots.append(root)
    roots = jnp.stack(roots, axis=1)
    len_r = lengths[r]
    positions = len_r[roots] + jnp.arange(steps, dtype=jnp.int32)[None, :]

    queries = rotate(qkv[..., :attn_width].reshape(beams, steps, Q_HEADS, head_dim), positions)
    new_keys = rotate(
        qkv[..., attn_width : attn_width + kv_width].reshape(beams, steps, KV_HEADS, head_dim),
        positions,
    )
    new_values = qkv[..., attn_width + kv_width :].reshape(beams, steps, KV_HEADS, head_dim)

    qg = queries.reshape(beams, steps, KV_HEADS, group, head_dim)
    score_parts = []
    for k in range(KV_HEADS):
        keys_k = cache_keys[:, :, k * head_dim : (k + 1) * head_dim]
        score_parts.append(
            jnp.einsum("btgd,cpd->cbtgp", qg[:, :, k], keys_k, preferred_element_type=jnp.float32)
        )
    scores = jnp.stack(score_parts, axis=3) * scale
    my_beams = j * owned + jnp.arange(owned, dtype=jnp.int32)
    limits = len_r[my_beams]
    live = (jnp.arange(context, dtype=jnp.int32)[None, :] < limits[:, None])[
        :, None, None, None, None, :
    ]
    scores = jnp.where(live, scores, masked_score)
    peak = jnp.max(scores, axis=-1)
    weights = jnp.where(live, jnp.exp(scores - peak[..., None]), 0.0)
    total = jnp.sum(weights, axis=-1)
    weights = weights.astype(jnp.bfloat16)
    output = jnp.stack(
        [
            jnp.einsum(
                "cbtgp,cpd->cbtgd",
                weights[:, :, :, k],
                cache_values[:, :, k * head_dim : (k + 1) * head_dim],
                preferred_element_type=jnp.float32,
            )
            for k in range(KV_HEADS)
        ],
        axis=3,
    )
    chosen = (roots[None, :, :] == my_beams[:, None, None])[..., None, None]
    peak = jnp.sum(jnp.where(chosen, peak, 0.0), axis=0)
    total = jnp.sum(jnp.where(chosen, total, 0.0), axis=0)
    output = jnp.sum(jnp.where(chosen[..., None], output, 0.0), axis=0)
    packed = jnp.concatenate([output, peak[..., None], total[..., None]], axis=-1)
    packed = packed.reshape(n_i, owned, steps, KV_HEADS, group, head_dim + 2)
    packed = lax.psum_scatter(packed, "tpi", scatter_dimension=0, tiled=True)[0]
    part_output = packed[..., :head_dim]
    part_peak = packed[..., head_dim]
    part_total = packed[..., head_dim + 1]

    anc = []
    for t in range(steps):
        cur = jnp.arange(beams, dtype=jnp.int32)
        row = [None] * steps
        row[t] = cur
        for step in range(t, 0, -1):
            cur = par[step][cur]
            row[step - 1] = cur
        for u in range(t + 1, steps):
            row[u] = jnp.arange(beams, dtype=jnp.int32)
        anc.append(jnp.stack(row, axis=0))
    anc = jnp.stack(anc, axis=0)
    anc_mine = lax.dynamic_slice_in_dim(anc, j * owned, owned, 2)
    anc_mine = jnp.transpose(anc_mine, (2, 0, 1))
    u_index = jnp.broadcast_to(jnp.arange(steps, dtype=jnp.int32), anc_mine.shape)
    hist_keys = new_keys[anc_mine, u_index]
    hist_values = new_values[anc_mine, u_index]
    q_mine = lax.dynamic_slice_in_dim(qg, j * owned, owned, 0)
    recent_scores = jnp.einsum(
        "ctkgd,ctukd->ctkgu", q_mine, hist_keys, preferred_element_type=jnp.float32
    ) * scale
    causal = (
        jnp.arange(steps, dtype=jnp.int32)[None, :] <= jnp.arange(steps, dtype=jnp.int32)[:, None]
    )[None, :, None, None, :]
    recent_scores = jnp.where(causal, recent_scores, masked_score)
    top = jnp.maximum(part_peak, jnp.max(recent_scores, axis=-1))
    factor = jnp.exp(part_peak - top)
    recent_weights = jnp.where(causal, jnp.exp(recent_scores - top[..., None]), 0.0)
    denominator = part_total * factor + jnp.sum(recent_weights, axis=-1)
    numerator = part_output * factor[..., None] + jnp.einsum(
        "ctkgu,ctukd->ctkgd",
        recent_weights.astype(jnp.bfloat16),
        hist_values,
        preferred_element_type=jnp.float32,
    )
    attention = (
        (numerator / denominator[..., None]).reshape(owned, steps, attn_width).astype(jnp.bfloat16)
    )

    att_all = lax.all_gather(attention, ALL, axis=0, tiled=True)
    my_requests = lax.dynamic_slice_in_dim(slot_request, req_index * group_requests, group_requests)
    att_group = att_all.reshape(requests, beams, steps, attn_width)[my_requests].reshape(
        group_rows, steps, attn_width
    )

    middle = x_group.astype(jnp.float32) + jnp.dot(
        att_group, full_out, preferred_element_type=jnp.float32
    )
    mixed_in = rms_normed(middle)
    gate = jnp.dot(mixed_in, gate_weight, preferred_element_type=jnp.float32)
    upward = jnp.dot(mixed_in, up_weight, preferred_element_type=jnp.float32)
    hidden = (jax.nn.silu(gate) * upward).astype(jnp.bfloat16)
    partial = jnp.dot(hidden, down_weight, preferred_element_type=jnp.float32).astype(jnp.bfloat16)
    chunk = rows_dev * steps * width
    partial = partial.reshape(tp_count, 16, chunk // 16)
    lowered = lax.psum_scatter(partial, TP, scatter_dimension=0, tiled=True)
    lowered = lowered.reshape(rows_dev, steps, width).astype(jnp.float32)
    middle_mine = lax.dynamic_slice_in_dim(middle, tp_index * rows_dev, rows_dev, 0)
    result = (middle_mine + lowered).astype(jnp.bfloat16)
    return jnp.swapaxes(result, 0, 1)


def solution(mesh):
    n_req = mesh.shape["req"]
    n_tp = mesh.shape["tp"]
    inner = 4
    devices = mesh.devices.reshape(n_req, n_tp // inner, inner)
    sub = Mesh(devices, ALL)
    rows = P(None, ALL, None)
    in_specs = (
        rows,
        P(),
        P(),
        P(TP, None),
        P(None, TP),
        P(None, TP),
        P(TP, None),
        P(ALL, None, None),
        P(ALL, None, None),
        P(),
        P(),
        P(),
    )
    return jax.shard_map(per_device, mesh=sub, in_specs=in_specs, out_specs=rows, check_vma=False)
```

```python
import jax
import jax.numpy as jnp
from jax import lax
from jax.sharding import Mesh
from jax.sharding import PartitionSpec as P

Q_HEADS = 12
KV_HEADS = 2

theta_base = 1000000.0
norm_eps = 1e-06
masked_score = -1e30

ALL = ("req", "tpo", "tpi")
TP = ("tpo", "tpi")


def rms_normed(values):
    values = values.astype(jnp.float32)
    factor = lax.rsqrt(jnp.mean(values * values, axis=-1, keepdims=True) + norm_eps)
    return (values * factor).astype(jnp.bfloat16)


def rotate(vectors, positions):
    half = vectors.shape[-1] // 2
    freqs = theta_base ** (-jnp.arange(half, dtype=jnp.float32) * 2.0 / vectors.shape[-1])
    angles = positions.astype(jnp.float32)[..., None] * freqs
    cosine = jnp.cos(angles)[..., None, :]
    sine = jnp.sin(angles)[..., None, :]
    values = vectors.astype(jnp.float32)
    first = values[..., :half]
    second = values[..., half:]
    return jnp.concatenate(
        [first * cosine - second * sine, second * cosine + first * sine], axis=-1
    ).astype(jnp.bfloat16)


def per_device(
    step_inputs,
    qkv_weight,
    qkv_bias,
    out_weight,
    gate_weight,
    up_weight,
    down_weight,
    cache_keys,
    cache_values,
    lengths,
    parents,
    slot_request,
):
    steps, rows_dev, width = step_inputs.shape
    beams = parents.shape[2]
    requests = slot_request.shape[0]
    n_req = lax.axis_size("req")
    n_o = lax.axis_size("tpo")
    n_i = lax.axis_size("tpi")
    tp_count = n_o * n_i
    group_requests = requests // n_req
    group_rows = group_requests * beams
    owned, context, kv_width = cache_keys.shape
    head_dim = kv_width // KV_HEADS
    group = Q_HEADS // KV_HEADS
    attn_width = Q_HEADS * head_dim
    scale = head_dim ** (-0.5)
    assert owned * n_i == beams

    req_index = lax.axis_index("req")
    tp_index = lax.axis_index("tpo") * n_i + lax.axis_index("tpi")
    j = lax.axis_index("tpi")
    flat = req_index * tp_count + tp_index
    r = flat // n_i

    inverse = (
        jnp.zeros((requests,), jnp.int32)
        .at[slot_request]
        .set(jnp.arange(requests, dtype=jnp.int32))
    )

    column_rows = out_weight.shape[0]
    share = column_rows // n_req
    w_share = lax.dynamic_slice_in_dim(out_weight, req_index * share, share, 0)
    carry = jnp.concatenate(
        [jnp.swapaxes(step_inputs, 0, 1).reshape(rows_dev * steps, width), w_share], axis=0
    )
    carry = lax.all_gather(carry, ALL, axis=0, tiled=False)
    x_all = carry[:, : rows_dev * steps].reshape(requests * beams, steps, width)
    full_out = (
        carry[:, rows_dev * steps :]
        .reshape(n_req, tp_count, share, width)
        .transpose(1, 0, 2, 3)
        .reshape(tp_count * column_rows, width)
    )
    x_req = lax.dynamic_slice_in_dim(x_all, inverse[r] * beams, beams, 0)
    x_group = lax.dynamic_slice_in_dim(x_all, req_index * group_rows, group_rows, 0)

    normed = rms_normed(x_req)
    qkv = (
        jnp.dot(normed, qkv_weight, preferred_element_type=jnp.float32) + qkv_bias
    ).astype(jnp.bfloat16)

    par = parents[:, r, :]
    root = jnp.arange(beams, dtype=jnp.int32)
    roots = []
    for t in range(steps):
        root = root[par[t]]
        roots.append(root)
    roots = jnp.stack(roots, axis=1)
    len_r = lengths[r]
    positions = len_r[roots] + jnp.arange(steps, dtype=jnp.int32)[None, :]

    queries = rotate(qkv[..., :attn_width].reshape(beams, steps, Q_HEADS, head_dim), positions)
    new_keys = rotate(
        qkv[..., attn_width : attn_width + kv_width].reshape(beams, steps, KV_HEADS, head_dim),
        positions,
    )
    new_values = qkv[..., attn_width + kv_width :].reshape(beams, steps, KV_HEADS, head_dim)

    qg = queries.reshape(beams, steps, KV_HEADS, group, head_dim)
    score_parts = []
    for k in range(KV_HEADS):
        keys_k = cache_keys[:, :, k * head_dim : (k + 1) * head_dim]
        score_parts.append(
            jnp.einsum("btgd,cpd->cbtgp", qg[:, :, k], keys_k, preferred_element_type=jnp.float32)
        )
    scores = jnp.stack(score_parts, axis=3) * scale
    my_beams = j * owned + jnp.arange(owned, dtype=jnp.int32)
    limits = len_r[my_beams]
    live = (jnp.arange(context, dtype=jnp.int32)[None, :] < limits[:, None])[
        :, None, None, None, None, :
    ]
    scores = jnp.where(live, scores, masked_score)
    peak = jnp.max(scores, axis=-1)
    weights = jnp.where(live, jnp.exp(scores - peak[..., None]), 0.0)
    total = jnp.sum(weights, axis=-1)
    weights = weights.astype(jnp.bfloat16)
    output = jnp.stack(
        [
            jnp.einsum(
                "cbtgp,cpd->cbtgd",
                weights[:, :, :, k],
                cache_values[:, :, k * head_dim : (k + 1) * head_dim],
                preferred_element_type=jnp.float32,
            )
            for k in range(KV_HEADS)
        ],
        axis=3,
    )
    chosen = (roots[None, :, :] == my_beams[:, None, None])[..., None, None]
    peak = jnp.sum(jnp.where(chosen, peak, 0.0), axis=0)
    total = jnp.sum(jnp.where(chosen, total, 0.0), axis=0)
    output = jnp.sum(jnp.where(chosen[..., None], output, 0.0), axis=0)
    part_output, part_peak, part_total = output, peak, total

    anc = []
    for t in range(steps):
        cur = jnp.arange(beams, dtype=jnp.int32)
        row = [None] * steps
        row[t] = cur
        for step in range(t, 0, -1):
            cur = par[step][cur]
            row[step - 1] = cur
        for u in range(t + 1, steps):
            row[u] = jnp.arange(beams, dtype=jnp.int32)
        anc.append(jnp.stack(row, axis=0))
    anc = jnp.transpose(jnp.stack(anc, axis=0), (2, 0, 1))
    u_index = jnp.broadcast_to(jnp.arange(steps, dtype=jnp.int32), anc.shape)
    hist_keys = new_keys[anc, u_index]
    hist_values = new_values[anc, u_index]
    recent_scores = jnp.einsum(
        "btkgd,btukd->btkgu", qg, hist_keys, preferred_element_type=jnp.float32
    ) * scale
    causal = (
        jnp.arange(steps, dtype=jnp.int32)[None, :] <= jnp.arange(steps, dtype=jnp.int32)[:, None]
    )[None, :, None, None, :]
    recent_scores = jnp.where(causal, recent_scores, masked_score)
    top = jnp.maximum(part_peak, jnp.max(recent_scores, axis=-1))
    factor = jnp.exp(part_peak - top)
    recent_weights = jnp.where(causal, jnp.exp(recent_scores - top[..., None]), 0.0)
    denominator = part_total * factor + jnp.sum(recent_weights, axis=-1)
    numerator = part_output * factor[..., None] + jnp.einsum(
        "btkgu,btukd->btkgd",
        recent_weights.astype(jnp.bfloat16),
        hist_values,
        preferred_element_type=jnp.float32,
    )
    attention = (
        (numerator / denominator[..., None]).reshape(beams, steps, attn_width).astype(jnp.bfloat16)
    )

    att_all = lax.all_gather(attention, ALL, axis=0, tiled=False)
    root_all = jnp.broadcast_to(jnp.arange(beams, dtype=jnp.int32), (requests, beams))
    root_steps = []
    for t in range(steps):
        root_all = jnp.take_along_axis(root_all, parents[t], axis=1)
        root_steps.append(root_all)
    root_steps = jnp.stack(root_steps, axis=2)
    my_requests = lax.dynamic_slice_in_dim(slot_request, req_index * group_requests, group_requests)
    source = my_requests[:, None, None] * n_i + root_steps[my_requests] // owned
    b_index = jnp.broadcast_to(jnp.arange(beams, dtype=jnp.int32)[None, :, None], source.shape)
    t_index = jnp.broadcast_to(jnp.arange(steps, dtype=jnp.int32)[None, None, :], source.shape)
    att_group = att_all[source, b_index, t_index].reshape(group_rows, steps, attn_width)

    middle = x_group.astype(jnp.float32) + jnp.dot(
        att_group, full_out, preferred_element_type=jnp.float32
    )
    mixed_in = rms_normed(middle)
    gate = jnp.dot(mixed_in, gate_weight, preferred_element_type=jnp.float32)
    upward = jnp.dot(mixed_in, up_weight, preferred_element_type=jnp.float32)
    hidden = (jax.nn.silu(gate) * upward).astype(jnp.bfloat16)
    partial = jnp.dot(hidden, down_weight, preferred_element_type=jnp.float32).astype(jnp.bfloat16)
    chunk = rows_dev * steps * width
    partial = partial.reshape(tp_count, 16, chunk // 16)
    lowered = lax.psum_scatter(partial, TP, scatter_dimension=0, tiled=True)
    lowered = lowered.reshape(rows_dev, steps, width).astype(jnp.float32)
    middle_mine = lax.dynamic_slice_in_dim(middle, tp_index * rows_dev, rows_dev, 0)
    result = (middle_mine + lowered).astype(jnp.bfloat16)
    return jnp.swapaxes(result, 0, 1)


def solution(mesh):
    n_req = mesh.shape["req"]
    n_tp = mesh.shape["tp"]
    inner = 4
    devices = mesh.devices.reshape(n_req, n_tp // inner, inner)
    sub = Mesh(devices, ALL)
    rows = P(None, ALL, None)
    in_specs = (
        rows,
        P(),
        P(),
        P(TP, None),
        P(None, TP),
        P(None, TP),
        P(TP, None),
        P(ALL, None, None),
        P(ALL, None, None),
        P(),
        P(),
        P(),
    )
    return jax.shard_map(per_device, mesh=sub, in_specs=in_specs, out_specs=rows, check_vma=False)
```

```python
import jax
import jax.numpy as jnp
from jax import lax
from jax.sharding import Mesh
from jax.sharding import PartitionSpec as P

Q_HEADS = 12
KV_HEADS = 2

theta_base = 1000000.0
norm_eps = 1e-06
masked_score = -1e30

ALL = ("req", "tpo", "tpi")
TP = ("tpo", "tpi")


def rms_normed(values):
    values = values.astype(jnp.float32)
    factor = lax.rsqrt(jnp.mean(values * values, axis=-1, keepdims=True) + norm_eps)
    return (values * factor).astype(jnp.bfloat16)


def rotate(vectors, positions):
    half = vectors.shape[-1] // 2
    freqs = theta_base ** (-jnp.arange(half, dtype=jnp.float32) * 2.0 / vectors.shape[-1])
    angles = positions.astype(jnp.float32)[..., None] * freqs
    cosine = jnp.cos(angles)[..., None, :]
    sine = jnp.sin(angles)[..., None, :]
    values = vectors.astype(jnp.float32)
    first = values[..., :half]
    second = values[..., half:]
    return jnp.concatenate(
        [first * cosine - second * sine, second * cosine + first * sine], axis=-1
    ).astype(jnp.bfloat16)


def per_device(
    step_inputs,
    qkv_weight,
    qkv_bias,
    out_weight,
    gate_weight,
    up_weight,
    down_weight,
    cache_keys,
    cache_values,
    lengths,
    parents,
    slot_request,
):
    steps, rows_dev, width = step_inputs.shape
    beams = parents.shape[2]
    requests = slot_request.shape[0]
    n_req = lax.axis_size("req")
    n_o = lax.axis_size("tpo")
    n_i = lax.axis_size("tpi")
    tp_count = n_o * n_i
    group_requests = requests // n_req
    group_rows = group_requests * beams
    owned, context, kv_width = cache_keys.shape
    head_dim = kv_width // KV_HEADS
    group = Q_HEADS // KV_HEADS
    attn_width = Q_HEADS * head_dim
    scale = head_dim ** (-0.5)
    assert owned * n_i == beams

    req_index = lax.axis_index("req")
    tp_index = lax.axis_index("tpo") * n_i + lax.axis_index("tpi")
    j = lax.axis_index("tpi")
    flat = req_index * tp_count + tp_index
    r = flat // n_i

    inverse = (
        jnp.zeros((requests,), jnp.int32)
        .at[slot_request]
        .set(jnp.arange(requests, dtype=jnp.int32))
    )

    column_rows = out_weight.shape[0]
    share = column_rows // n_req
    w_share = lax.dynamic_slice_in_dim(out_weight, req_index * share, share, 0)
    carry = jnp.concatenate(
        [jnp.swapaxes(step_inputs, 0, 1).reshape(rows_dev * steps, width), w_share], axis=0
    )
    carry = lax.all_gather(carry, ALL, axis=0, tiled=False)
    x_all = carry[:, : rows_dev * steps].reshape(requests * beams, steps, width)
    full_out = (
        carry[:, rows_dev * steps :]
        .reshape(n_req, tp_count, share, width)
        .transpose(1, 0, 2, 3)
        .reshape(tp_count * column_rows, width)
    )
    x_req = lax.dynamic_slice_in_dim(x_all, inverse[r] * beams, beams, 0)
    x_group = lax.dynamic_slice_in_dim(x_all, req_index * group_rows, group_rows, 0)

    normed = rms_normed(x_req)
    qkv = (
        jnp.dot(normed, qkv_weight, preferred_element_type=jnp.float32) + qkv_bias
    ).astype(jnp.bfloat16)

    par = parents[:, r, :]
    root = jnp.arange(beams, dtype=jnp.int32)
    roots = []
    for t in range(steps):
        root = root[par[t]]
        roots.append(root)
    roots = jnp.stack(roots, axis=1)
    len_r = lengths[r]
    positions = len_r[roots] + jnp.arange(steps, dtype=jnp.int32)[None, :]

    queries = rotate(qkv[..., :attn_width].reshape(beams, steps, Q_HEADS, head_dim), positions)
    new_keys = rotate(
        qkv[..., attn_width : attn_width + kv_width].reshape(beams, steps, KV_HEADS, head_dim),
        positions,
    )
    new_values = qkv[..., attn_width + kv_width :].reshape(beams, steps, KV_HEADS, head_dim)

    qg = queries.reshape(beams, steps, KV_HEADS, group, head_dim)
    score_parts = []
    for k in range(KV_HEADS):
        keys_k = cache_keys[:, :, k * head_dim : (k + 1) * head_dim]
        score_parts.append(
            jnp.einsum("btgd,cpd->cbtgp", qg[:, :, k], keys_k, preferred_element_type=jnp.float32)
        )
    scores = jnp.stack(score_parts, axis=3) * scale
    my_beams = j * owned + jnp.arange(owned, dtype=jnp.int32)
    limits = len_r[my_beams]
    live = (jnp.arange(context, dtype=jnp.int32)[None, :] < limits[:, None])[
        :, None, None, None, None, :
    ]
    scores = jnp.where(live, scores, masked_score)
    peak = jnp.max(scores, axis=-1)
    weights = jnp.where(live, jnp.exp(scores - peak[..., None]), 0.0)
    total = jnp.sum(weights, axis=-1)
    weights = weights.astype(jnp.bfloat16)
    output = jnp.stack(
        [
            jnp.einsum(
                "cbtgp,cpd->cbtgd",
                weights[:, :, :, k],
                cache_values[:, :, k * head_dim : (k + 1) * head_dim],
                preferred_element_type=jnp.float32,
            )
            for k in range(KV_HEADS)
        ],
        axis=3,
    )
    chosen = (roots[None, :, :] == my_beams[:, None, None])[..., None, None]
    peak = jnp.sum(jnp.where(chosen, peak, 0.0), axis=0)
    total = jnp.sum(jnp.where(chosen, total, 0.0), axis=0)
    output = jnp.sum(jnp.where(chosen[..., None], output, 0.0), axis=0)
    packed = jnp.concatenate([output, peak[..., None], total[..., None]], axis=-1)
    packed = packed.reshape(n_i, owned, steps, KV_HEADS, group, head_dim + 2)
    packed = lax.psum_scatter(packed, "tpi", scatter_dimension=0, tiled=True)[0]
    part_output = packed[..., :head_dim]
    part_peak = packed[..., head_dim]
    part_total = packed[..., head_dim + 1]

    anc = []
    for t in range(steps):
        cur = jnp.arange(beams, dtype=jnp.int32)
        row = [None] * steps
        row[t] = cur
        for step in range(t, 0, -1):
            cur = par[step][cur]
            row[step - 1] = cur
        for u in range(t + 1, steps):
            row[u] = jnp.arange(beams, dtype=jnp.int32)
        anc.append(jnp.stack(row, axis=0))
    anc = jnp.stack(anc, axis=0)
    anc_mine = lax.dynamic_slice_in_dim(anc, j * owned, owned, 2)
    anc_mine = jnp.transpose(anc_mine, (2, 0, 1))
    u_index = jnp.broadcast_to(jnp.arange(steps, dtype=jnp.int32), anc_mine.shape)
    hist_keys = new_keys[anc_mine, u_index]
    hist_values = new_values[anc_mine, u_index]
    q_mine = lax.dynamic_slice_in_dim(qg, j * owned, owned, 0)
    recent_scores = jnp.einsum(
        "ctkgd,ctukd->ctkgu", q_mine, hist_keys, preferred_element_type=jnp.float32
    ) * scale
    causal = (
        jnp.arange(steps, dtype=jnp.int32)[None, :] <= jnp.arange(steps, dtype=jnp.int32)[:, None]
    )[None, :, None, None, :]
    recent_scores = jnp.where(causal, recent_scores, masked_score)
    top = jnp.maximum(part_peak, jnp.max(recent_scores, axis=-1))
    factor = jnp.exp(part_peak - top)
    recent_weights = jnp.where(causal, jnp.exp(recent_scores - top[..., None]), 0.0)
    denominator = part_total * factor + jnp.sum(recent_weights, axis=-1)
    numerator = part_output * factor[..., None] + jnp.einsum(
        "ctkgu,ctukd->ctkgd",
        recent_weights.astype(jnp.bfloat16),
        hist_values,
        preferred_element_type=jnp.float32,
    )
    attention = (
        (numerator / denominator[..., None]).reshape(owned, steps, attn_width).astype(jnp.bfloat16)
    )

    att_all = lax.all_gather(attention, ALL, axis=0, tiled=True)
    my_requests = lax.dynamic_slice_in_dim(slot_request, req_index * group_requests, group_requests)
    att_group = att_all.reshape(requests, beams, steps, attn_width)[my_requests].reshape(
        group_rows, steps, attn_width
    )

    middle = x_group.astype(jnp.float32) + jnp.dot(
        att_group, full_out, preferred_element_type=jnp.float32
    )
    mixed_in = rms_normed(middle)
    gate = jnp.dot(mixed_in, gate_weight, preferred_element_type=jnp.float32)
    upward = jnp.dot(mixed_in, up_weight, preferred_element_type=jnp.float32)
    hidden = (jax.nn.silu(gate) * upward).astype(jnp.bfloat16)
    partial = jnp.dot(hidden, down_weight, preferred_element_type=jnp.float32).astype(jnp.bfloat16)
    partial = partial.reshape(n_o, n_i, rows_dev * steps, width)
    partial = jnp.swapaxes(partial, 0, 1).reshape(n_i, n_o * rows_dev * steps, width)
    partial = lax.psum_scatter(partial, "tpi", scatter_dimension=0, tiled=True)
    partial = partial.reshape(n_o, 16, rows_dev * steps * width // 16)
    lowered = lax.psum_scatter(partial, "tpo", scatter_dimension=0, tiled=True)
    lowered = lowered.reshape(rows_dev, steps, width).astype(jnp.float32)
    middle_mine = lax.dynamic_slice_in_dim(middle, tp_index * rows_dev, rows_dev, 0)
    result = (middle_mine + lowered).astype(jnp.bfloat16)
    return jnp.swapaxes(result, 0, 1)


def solution(mesh):
    n_req = mesh.shape["req"]
    n_tp = mesh.shape["tp"]
    inner = 4
    devices = mesh.devices.reshape(n_req, n_tp // inner, inner)
    sub = Mesh(devices, ALL)
    rows = P(None, ALL, None)
    in_specs = (
        rows,
        P(),
        P(),
        P(TP, None),
        P(None, TP),
        P(None, TP),
        P(TP, None),
        P(ALL, None, None),
        P(ALL, None, None),
        P(),
        P(),
        P(),
    )
    return jax.shard_map(per_device, mesh=sub, in_specs=in_specs, out_specs=rows, check_vma=False)
```

```python
import jax
import jax.numpy as jnp
from jax import lax
from jax.sharding import Mesh
from jax.sharding import PartitionSpec as P

Q_HEADS = 12
KV_HEADS = 2

theta_base = 1000000.0
norm_eps = 1e-06
masked_score = -1e30

ALL = ("req", "tpo", "tpi")
TP = ("tpo", "tpi")


def rms_normed(values):
    values = values.astype(jnp.float32)
    factor = lax.rsqrt(jnp.mean(values * values, axis=-1, keepdims=True) + norm_eps)
    return (values * factor).astype(jnp.bfloat16)


def rotate(vectors, positions):
    half = vectors.shape[-1] // 2
    freqs = theta_base ** (-jnp.arange(half, dtype=jnp.float32) * 2.0 / vectors.shape[-1])
    angles = positions.astype(jnp.float32)[..., None] * freqs
    cosine = jnp.cos(angles)[..., None, :]
    sine = jnp.sin(angles)[..., None, :]
    values = vectors.astype(jnp.float32)
    first = values[..., :half]
    second = values[..., half:]
    return jnp.concatenate(
        [first * cosine - second * sine, second * cosine + first * sine], axis=-1
    ).astype(jnp.bfloat16)


def per_device(
    step_inputs,
    qkv_weight,
    qkv_bias,
    out_weight,
    gate_weight,
    up_weight,
    down_weight,
    cache_keys,
    cache_values,
    lengths,
    parents,
    slot_request,
):
    steps, rows_dev, width = step_inputs.shape
    beams = parents.shape[2]
    requests = slot_request.shape[0]
    n_req = lax.axis_size("req")
    n_o = lax.axis_size("tpo")
    n_i = lax.axis_size("tpi")
    tp_count = n_o * n_i
    group_requests = requests // n_req
    group_rows = group_requests * beams
    owned, context, kv_width = cache_keys.shape
    head_dim = kv_width // KV_HEADS
    group = Q_HEADS // KV_HEADS
    attn_width = Q_HEADS * head_dim
    scale = head_dim ** (-0.5)
    assert owned * n_i == beams

    req_index = lax.axis_index("req")
    tp_index = lax.axis_index("tpo") * n_i + lax.axis_index("tpi")
    j = lax.axis_index("tpi")
    flat = req_index * tp_count + tp_index
    r = flat // n_i

    inverse = (
        jnp.zeros((requests,), jnp.int32)
        .at[slot_request]
        .set(jnp.arange(requests, dtype=jnp.int32))
    )

    column_rows = out_weight.shape[0]
    share = column_rows // n_req
    w_share = lax.dynamic_slice_in_dim(out_weight, req_index * share, share, 0)
    carry = jnp.concatenate(
        [jnp.swapaxes(step_inputs, 0, 1).reshape(rows_dev * steps, width), w_share], axis=0
    )
    carry = lax.all_gather(carry, ALL, axis=0, tiled=False)
    x_all = carry[:, : rows_dev * steps].reshape(requests * beams, steps, width)
    full_out = (
        carry[:, rows_dev * steps :]
        .reshape(n_req, tp_count, share, width)
        .transpose(1, 0, 2, 3)
        .reshape(tp_count * column_rows, width)
    )
    x_req = lax.dynamic_slice_in_dim(x_all, inverse[r] * beams, beams, 0)
    x_group = lax.dynamic_slice_in_dim(x_all, req_index * group_rows, group_rows, 0)

    normed = rms_normed(x_req)
    qkv = (
        jnp.dot(normed, qkv_weight, preferred_element_type=jnp.float32) + qkv_bias
    ).astype(jnp.bfloat16)

    par = parents[:, r, :]
    root = jnp.arange(beams, dtype=jnp.int32)
    roots = []
    for t in range(steps):
        root = root[par[t]]
        roots.append(root)
    roots = jnp.stack(roots, axis=1)
    len_r = lengths[r]
    positions = len_r[roots] + jnp.arange(steps, dtype=jnp.int32)[None, :]

    queries = rotate(qkv[..., :attn_width].reshape(beams, steps, Q_HEADS, head_dim), positions)
    new_keys = rotate(
        qkv[..., attn_width : attn_width + kv_width].reshape(beams, steps, KV_HEADS, head_dim),
        positions,
    )
    new_values = qkv[..., attn_width + kv_width :].reshape(beams, steps, KV_HEADS, head_dim)

    qg = queries.reshape(beams, steps, KV_HEADS, group, head_dim)
    score_parts = []
    for k in range(KV_HEADS):
        keys_k = cache_keys[:, :, k * head_dim : (k + 1) * head_dim]
        score_parts.append(
            jnp.einsum("btgd,cpd->cbtgp", qg[:, :, k], keys_k, preferred_element_type=jnp.float32)
        )
    scores = jnp.stack(score_parts, axis=3) * scale
    my_beams = j * owned + jnp.arange(owned, dtype=jnp.int32)
    limits = len_r[my_beams]
    live = (jnp.arange(context, dtype=jnp.int32)[None, :] < limits[:, None])[
        :, None, None, None, None, :
    ]
    scores = jnp.where(live, scores, masked_score)
    peak = jnp.max(scores, axis=-1)
    weights = jnp.where(live, jnp.exp(scores - peak[..., None]), 0.0)
    total = jnp.sum(weights, axis=-1)
    weights = weights.astype(jnp.bfloat16)
    output = jnp.stack(
        [
            jnp.einsum(
                "cbtgp,cpd->cbtgd",
                weights[:, :, :, k],
                cache_values[:, :, k * head_dim : (k + 1) * head_dim],
                preferred_element_type=jnp.float32,
            )
            for k in range(KV_HEADS)
        ],
        axis=3,
    )
    chosen = (roots[None, :, :] == my_beams[:, None, None])[..., None, None]
    peak = jnp.sum(jnp.where(chosen, peak, 0.0), axis=0)
    total = jnp.sum(jnp.where(chosen, total, 0.0), axis=0)
    output = jnp.sum(jnp.where(chosen[..., None], output, 0.0), axis=0)
    packed = jnp.concatenate([output, peak[..., None], total[..., None]], axis=-1)
    packed = packed.reshape(n_i, owned, steps, KV_HEADS, group, head_dim + 2)
    packed = lax.psum_scatter(packed, "tpi", scatter_dimension=0, tiled=True)[0]
    part_output = packed[..., :head_dim]
    part_peak = packed[..., head_dim]
    part_total = packed[..., head_dim + 1]

    anc = []
    for t in range(steps):
        cur = jnp.arange(beams, dtype=jnp.int32)
        row = [None] * steps
        row[t] = cur
        for step in range(t, 0, -1):
            cur = par[step][cur]
            row[step - 1] = cur
        for u in range(t + 1, steps):
            row[u] = jnp.arange(beams, dtype=jnp.int32)
        anc.append(jnp.stack(row, axis=0))
    anc = jnp.stack(anc, axis=0)
    anc_mine = lax.dynamic_slice_in_dim(anc, j * owned, owned, 2)
    anc_mine = jnp.transpose(anc_mine, (2, 0, 1))
    u_index = jnp.broadcast_to(jnp.arange(steps, dtype=jnp.int32), anc_mine.shape)
    hist_keys = new_keys[anc_mine, u_index]
    hist_values = new_values[anc_mine, u_index]
    q_mine = lax.dynamic_slice_in_dim(qg, j * owned, owned, 0)
    recent_scores = jnp.einsum(
        "ctkgd,ctukd->ctkgu", q_mine, hist_keys, preferred_element_type=jnp.float32
    ) * scale
    causal = (
        jnp.arange(steps, dtype=jnp.int32)[None, :] <= jnp.arange(steps, dtype=jnp.int32)[:, None]
    )[None, :, None, None, :]
    recent_scores = jnp.where(causal, recent_scores, masked_score)
    top = jnp.maximum(part_peak, jnp.max(recent_scores, axis=-1))
    factor = jnp.exp(part_peak - top)
    recent_weights = jnp.where(causal, jnp.exp(recent_scores - top[..., None]), 0.0)
    denominator = part_total * factor + jnp.sum(recent_weights, axis=-1)
    numerator = part_output * factor[..., None] + jnp.einsum(
        "ctkgu,ctukd->ctkgd",
        recent_weights.astype(jnp.bfloat16),
        hist_values,
        preferred_element_type=jnp.float32,
    )
    attention = (
        (numerator / denominator[..., None]).reshape(owned, steps, attn_width).astype(jnp.bfloat16)
    )

    att_all = lax.all_gather(attention, ALL, axis=0, tiled=True)
    my_requests = lax.dynamic_slice_in_dim(slot_request, req_index * group_requests, group_requests)
    att_group = att_all.reshape(requests, beams, steps, attn_width)[my_requests].reshape(
        group_rows, steps, attn_width
    )

    middle = x_group.astype(jnp.float32) + jnp.dot(
        att_group, full_out, preferred_element_type=jnp.float32
    )
    mixed_in = rms_normed(middle)
    gate = jnp.dot(mixed_in, gate_weight, preferred_element_type=jnp.float32)
    upward = jnp.dot(mixed_in, up_weight, preferred_element_type=jnp.float32)
    hidden = (jax.nn.silu(gate) * upward).astype(jnp.bfloat16)
    partial = jnp.dot(hidden, down_weight, preferred_element_type=jnp.float32)
    partial = partial.reshape(tp_count, rows_dev * steps, width)
    bit = 1
    while bit < tp_count:
        pairs = partial.reshape(partial.shape[0] // 2, 2, rows_dev * steps, width)
        mine = (tp_index // bit) % 2
        keep = jnp.where(mine == 0, pairs[:, 0], pairs[:, 1])
        send = jnp.where(mine == 0, pairs[:, 1], pairs[:, 0])
        perm = [(i, i ^ bit) for i in range(tp_count)]
        partial = keep + lax.ppermute(send, TP, perm)
        bit *= 2
    lowered = partial.reshape(rows_dev, steps, width)
    middle_mine = lax.dynamic_slice_in_dim(middle, tp_index * rows_dev, rows_dev, 0)
    result = (middle_mine + lowered).astype(jnp.bfloat16)
    return jnp.swapaxes(result, 0, 1)


def solution(mesh):
    n_req = mesh.shape["req"]
    n_tp = mesh.shape["tp"]
    inner = 4
    devices = mesh.devices.reshape(n_req, n_tp // inner, inner)
    sub = Mesh(devices, ALL)
    rows = P(None, ALL, None)
    in_specs = (
        rows,
        P(),
        P(),
        P(TP, None),
        P(None, TP),
        P(None, TP),
        P(TP, None),
        P(ALL, None, None),
        P(ALL, None, None),
        P(),
        P(),
        P(),
    )
    return jax.shard_map(per_device, mesh=sub, in_specs=in_specs, out_specs=rows, check_vma=False)
```

```python
import jax
import jax.numpy as jnp
from jax import lax
from jax.sharding import Mesh
from jax.sharding import PartitionSpec as P

Q_HEADS = 12
KV_HEADS = 2

theta_base = 1000000.0
norm_eps = 1e-06
masked_score = -1e30

ALL = ("req", "tpo", "tpi")
TP = ("tpo", "tpi")


def rms_normed(values):
    values = values.astype(jnp.float32)
    factor = lax.rsqrt(jnp.mean(values * values, axis=-1, keepdims=True) + norm_eps)
    return (values * factor).astype(jnp.bfloat16)


def rotate(vectors, positions):
    half = vectors.shape[-1] // 2
    freqs = theta_base ** (-jnp.arange(half, dtype=jnp.float32) * 2.0 / vectors.shape[-1])
    angles = positions.astype(jnp.float32)[..., None] * freqs
    cosine = jnp.cos(angles)[..., None, :]
    sine = jnp.sin(angles)[..., None, :]
    values = vectors.astype(jnp.float32)
    first = values[..., :half]
    second = values[..., half:]
    return jnp.concatenate(
        [first * cosine - second * sine, second * cosine + first * sine], axis=-1
    ).astype(jnp.bfloat16)


def gather_rounds(x, axes, index, masks):
    count = 1 << len(masks)
    buf = x
    bits = []
    for mask in masks:
        low = mask & (-mask)
        bit = low if mask == low else mask - low
        perm = [(i, i ^ mask) for i in range(count)]
        recv = lax.ppermute(buf, axes, perm)
        mine = (index // bit) % 2
        buf = jnp.where(mine == 0, jnp.stack([buf, recv]), jnp.stack([recv, buf]))
        bits.append(bit)
    depth = len(bits)
    order = sorted(range(depth), key=lambda a: -bits[depth - 1 - a])
    buf = jnp.transpose(buf, tuple(order) + tuple(range(depth, buf.ndim)))
    return buf.reshape((count,) + x.shape)


def scatter_rounds(x, axes, index):
    count = x.shape[0]
    buf = x
    bit = 1
    while bit < count:
        pairs = buf.reshape((buf.shape[0] // 2, 2) + buf.shape[1:])
        mine = (index // bit) % 2
        keep = jnp.where(mine == 0, pairs[:, 0], pairs[:, 1])
        send = jnp.where(mine == 0, pairs[:, 1], pairs[:, 0])
        perm = [(i, i ^ bit) for i in range(count)]
        buf = keep + lax.ppermute(send, axes, perm)
        bit *= 2
    return buf[0]


def gather_masks(n_req, tp_count):
    masks = []
    for shift, size in ((tp_count.bit_length() - 1, n_req), (3, 4), (1, 4)):
        low = 1 << shift
        masks.append(low)
        if size == 4:
            masks.append(3 * low)
    masks.append(1)
    return masks


def per_device(
    step_inputs,
    qkv_weight,
    qkv_bias,
    out_weight,
    gate_weight,
    up_weight,
    down_weight,
    cache_keys,
    cache_values,
    lengths,
    parents,
    slot_request,
):
    steps, rows_dev, width = step_inputs.shape
    beams = parents.shape[2]
    requests = slot_request.shape[0]
    n_req = lax.axis_size("req")
    n_o = lax.axis_size("tpo")
    n_i = lax.axis_size("tpi")
    tp_count = n_o * n_i
    group_requests = requests // n_req
    group_rows = group_requests * beams
    owned, context, kv_width = cache_keys.shape
    head_dim = kv_width // KV_HEADS
    group = Q_HEADS // KV_HEADS
    attn_width = Q_HEADS * head_dim
    scale = head_dim ** (-0.5)
    assert owned * n_i == beams

    req_index = lax.axis_index("req")
    tp_index = lax.axis_index("tpo") * n_i + lax.axis_index("tpi")
    j = lax.axis_index("tpi")
    flat = req_index * tp_count + tp_index
    r = flat // n_i

    inverse = (
        jnp.zeros((requests,), jnp.int32)
        .at[slot_request]
        .set(jnp.arange(requests, dtype=jnp.int32))
    )

    flat_masks = gather_masks(n_req, tp_count)
    x_all = gather_rounds(
        jnp.swapaxes(step_inputs, 0, 1).reshape(rows_dev * steps, width), ALL, flat, flat_masks
    ).reshape(requests * beams, steps, width)
    full_out = lax.all_gather(out_weight, TP, axis=0, tiled=True)
    x_req = lax.dynamic_slice_in_dim(x_all, inverse[r] * beams, beams, 0)
    x_group = lax.dynamic_slice_in_dim(x_all, req_index * group_rows, group_rows, 0)

    normed = rms_normed(x_req)
    qkv = (
        jnp.dot(normed, qkv_weight, preferred_element_type=jnp.float32) + qkv_bias
    ).astype(jnp.bfloat16)

    par = parents[:, r, :]
    root = jnp.arange(beams, dtype=jnp.int32)
    roots = []
    for t in range(steps):
        root = root[par[t]]
        roots.append(root)
    roots = jnp.stack(roots, axis=1)
    len_r = lengths[r]
    positions = len_r[roots] + jnp.arange(steps, dtype=jnp.int32)[None, :]

    queries = rotate(qkv[..., :attn_width].reshape(beams, steps, Q_HEADS, head_dim), positions)
    new_keys = rotate(
        qkv[..., attn_width : attn_width + kv_width].reshape(beams, steps, KV_HEADS, head_dim),
        positions,
    )
    new_values = qkv[..., attn_width + kv_width :].reshape(beams, steps, KV_HEADS, head_dim)

    qg = queries.reshape(beams, steps, KV_HEADS, group, head_dim)
    score_parts = []
    for k in range(KV_HEADS):
        keys_k = cache_keys[:, :, k * head_dim : (k + 1) * head_dim]
        score_parts.append(
            jnp.einsum("btgd,cpd->cbtgp", qg[:, :, k], keys_k, preferred_element_type=jnp.float32)
        )
    scores = jnp.stack(score_parts, axis=3) * scale
    my_beams = j * owned + jnp.arange(owned, dtype=jnp.int32)
    limits = len_r[my_beams]
    live = (jnp.arange(context, dtype=jnp.int32)[None, :] < limits[:, None])[
        :, None, None, None, None, :
    ]
    scores = jnp.where(live, scores, masked_score)
    peak = jnp.max(scores, axis=-1)
    weights = jnp.where(live, jnp.exp(scores - peak[..., None]), 0.0)
    total = jnp.sum(weights, axis=-1)
    weights = weights.astype(jnp.bfloat16)
    output = jnp.stack(
        [
            jnp.einsum(
                "cbtgp,cpd->cbtgd",
                weights[:, :, :, k],
                cache_values[:, :, k * head_dim : (k + 1) * head_dim],
                preferred_element_type=jnp.float32,
            )
            for k in range(KV_HEADS)
        ],
        axis=3,
    )
    chosen = (roots[None, :, :] == my_beams[:, None, None])[..., None, None]
    peak = jnp.sum(jnp.where(chosen, peak, 0.0), axis=0)
    total = jnp.sum(jnp.where(chosen, total, 0.0), axis=0)
    output = jnp.sum(jnp.where(chosen[..., None], output, 0.0), axis=0)
    packed = jnp.concatenate([output, peak[..., None], total[..., None]], axis=-1)
    packed = packed.reshape(n_i, owned, steps, KV_HEADS, group, head_dim + 2)
    packed = scatter_rounds(packed, "tpi", j)
    part_output = packed[..., :head_dim]
    part_peak = packed[..., head_dim]
    part_total = packed[..., head_dim + 1]

    anc = []
    for t in range(steps):
        cur = jnp.arange(beams, dtype=jnp.int32)
        row = [None] * steps
        row[t] = cur
        for step in range(t, 0, -1):
            cur = par[step][cur]
            row[step - 1] = cur
        for u in range(t + 1, steps):
            row[u] = jnp.arange(beams, dtype=jnp.int32)
        anc.append(jnp.stack(row, axis=0))
    anc = jnp.stack(anc, axis=0)
    anc_mine = lax.dynamic_slice_in_dim(anc, j * owned, owned, 2)
    anc_mine = jnp.transpose(anc_mine, (2, 0, 1))
    u_index = jnp.broadcast_to(jnp.arange(steps, dtype=jnp.int32), anc_mine.shape)
    hist_keys = new_keys[anc_mine, u_index]
    hist_values = new_values[anc_mine, u_index]
    q_mine = lax.dynamic_slice_in_dim(qg, j * owned, owned, 0)
    recent_scores = jnp.einsum(
        "ctkgd,ctukd->ctkgu", q_mine, hist_keys, preferred_element_type=jnp.float32
    ) * scale
    causal = (
        jnp.arange(steps, dtype=jnp.int32)[None, :] <= jnp.arange(steps, dtype=jnp.int32)[:, None]
    )[None, :, None, None, :]
    recent_scores = jnp.where(causal, recent_scores, masked_score)
    top = jnp.maximum(part_peak, jnp.max(recent_scores, axis=-1))
    factor = jnp.exp(part_peak - top)
    recent_weights = jnp.where(causal, jnp.exp(recent_scores - top[..., None]), 0.0)
    denominator = part_total * factor + jnp.sum(recent_weights, axis=-1)
    numerator = part_output * factor[..., None] + jnp.einsum(
        "ctkgu,ctukd->ctkgd",
        recent_weights.astype(jnp.bfloat16),
        hist_values,
        preferred_element_type=jnp.float32,
    )
    attention = (
        (numerator / denominator[..., None]).reshape(owned, steps, attn_width).astype(jnp.bfloat16)
    )

    att_all = gather_rounds(attention, ALL, flat, flat_masks).reshape(
        requests * beams, steps, attn_width
    )
    my_requests = lax.dynamic_slice_in_dim(slot_request, req_index * group_requests, group_requests)
    att_group = att_all.reshape(requests, beams, steps, attn_width)[my_requests].reshape(
        group_rows, steps, attn_width
    )

    middle = x_group.astype(jnp.float32) + jnp.dot(
        att_group, full_out, preferred_element_type=jnp.float32
    )
    mixed_in = rms_normed(middle)
    gate = jnp.dot(mixed_in, gate_weight, preferred_element_type=jnp.float32)
    upward = jnp.dot(mixed_in, up_weight, preferred_element_type=jnp.float32)
    hidden = (jax.nn.silu(gate) * upward).astype(jnp.bfloat16)
    partial = jnp.dot(hidden, down_weight, preferred_element_type=jnp.float32)
    partial = scatter_rounds(partial.reshape(tp_count, rows_dev * steps, width), TP, tp_index)
    lowered = partial.reshape(rows_dev, steps, width)
    middle_mine = lax.dynamic_slice_in_dim(middle, tp_index * rows_dev, rows_dev, 0)
    result = (middle_mine + lowered).astype(jnp.bfloat16)
    return jnp.swapaxes(result, 0, 1)


def solution(mesh):
    n_req = mesh.shape["req"]
    n_tp = mesh.shape["tp"]
    inner = 4
    devices = mesh.devices.reshape(n_req, n_tp // inner, inner)
    sub = Mesh(devices, ALL)
    rows = P(None, ALL, None)
    in_specs = (
        rows,
        P(),
        P(),
        P(TP, None),
        P(None, TP),
        P(None, TP),
        P(TP, None),
        P(ALL, None, None),
        P(ALL, None, None),
        P(),
        P(),
        P(),
    )
    return jax.shard_map(per_device, mesh=sub, in_specs=in_specs, out_specs=rows, check_vma=False)
```

```python
import jax
import jax.numpy as jnp
from jax import lax
from jax.sharding import Mesh
from jax.sharding import PartitionSpec as P

Q_HEADS = 12
KV_HEADS = 2

theta_base = 1000000.0
norm_eps = 1e-06
masked_score = -1e30

ALL = ("req", "tpo", "tpi")
TP = ("tpo", "tpi")


def rms_normed(values):
    values = values.astype(jnp.float32)
    factor = lax.rsqrt(jnp.mean(values * values, axis=-1, keepdims=True) + norm_eps)
    return (values * factor).astype(jnp.bfloat16)


def rotate(vectors, positions):
    half = vectors.shape[-1] // 2
    freqs = theta_base ** (-jnp.arange(half, dtype=jnp.float32) * 2.0 / vectors.shape[-1])
    angles = positions.astype(jnp.float32)[..., None] * freqs
    cosine = jnp.cos(angles)[..., None, :]
    sine = jnp.sin(angles)[..., None, :]
    values = vectors.astype(jnp.float32)
    first = values[..., :half]
    second = values[..., half:]
    return jnp.concatenate(
        [first * cosine - second * sine, second * cosine + first * sine], axis=-1
    ).astype(jnp.bfloat16)


def gather_rounds(x, axes, index, masks):
    count = 1 << len(masks)
    buf = x
    bits = []
    for mask in masks:
        low = mask & (-mask)
        bit = low if mask == low else mask - low
        perm = [(i, i ^ mask) for i in range(count)]
        recv = lax.ppermute(buf, axes, perm)
        mine = (index // bit) % 2
        buf = jnp.where(mine == 0, jnp.stack([buf, recv]), jnp.stack([recv, buf]))
        bits.append(bit)
    depth = len(bits)
    order = sorted(range(depth), key=lambda a: -bits[depth - 1 - a])
    buf = jnp.transpose(buf, tuple(order) + tuple(range(depth, buf.ndim)))
    return buf.reshape((count,) + x.shape)


def scatter_rounds(x, axes, index):
    count = x.shape[0]
    buf = x
    bit = 1
    while bit < count:
        pairs = buf.reshape((buf.shape[0] // 2, 2) + buf.shape[1:])
        mine = (index // bit) % 2
        keep = jnp.where(mine == 0, pairs[:, 0], pairs[:, 1])
        send = jnp.where(mine == 0, pairs[:, 1], pairs[:, 0])
        perm = [(i, i ^ bit) for i in range(count)]
        buf = keep + lax.ppermute(send, axes, perm)
        bit *= 2
    return buf[0]


def gather_masks(n_req, tp_count):
    masks = []
    for shift, size in ((tp_count.bit_length() - 1, n_req), (3, 4), (1, 4)):
        low = 1 << shift
        masks.append(low)
        if size == 4:
            masks.append(3 * low)
    masks.append(1)
    return masks


def per_device(
    step_inputs,
    qkv_weight,
    qkv_bias,
    out_weight,
    gate_weight,
    up_weight,
    down_weight,
    cache_keys,
    cache_values,
    lengths,
    parents,
    slot_request,
):
    steps, rows_dev, width = step_inputs.shape
    beams = parents.shape[2]
    requests = slot_request.shape[0]
    n_req = lax.axis_size("req")
    n_o = lax.axis_size("tpo")
    n_i = lax.axis_size("tpi")
    tp_count = n_o * n_i
    group_requests = requests // n_req
    group_rows = group_requests * beams
    owned, context, kv_width = cache_keys.shape
    head_dim = kv_width // KV_HEADS
    group = Q_HEADS // KV_HEADS
    attn_width = Q_HEADS * head_dim
    scale = head_dim ** (-0.5)
    assert owned * n_i == beams

    req_index = lax.axis_index("req")
    tp_index = lax.axis_index("tpo") * n_i + lax.axis_index("tpi")
    j = lax.axis_index("tpi")
    flat = req_index * tp_count + tp_index
    r = flat // n_i

    inverse = (
        jnp.zeros((requests,), jnp.int32)
        .at[slot_request]
        .set(jnp.arange(requests, dtype=jnp.int32))
    )

    flat_masks = gather_masks(n_req, tp_count)
    x_all = gather_rounds(
        jnp.swapaxes(step_inputs, 0, 1).reshape(rows_dev * steps, width), ALL, flat, flat_masks
    ).reshape(requests * beams, steps, width)
    after_rows = (x_all[0, 0, 0] * 0).astype(out_weight.dtype)
    full_out = lax.all_gather(out_weight + after_rows, TP, axis=0, tiled=True)
    x_req = lax.dynamic_slice_in_dim(x_all, inverse[r] * beams, beams, 0)
    x_group = lax.dynamic_slice_in_dim(x_all, req_index * group_rows, group_rows, 0)

    normed = rms_normed(x_req)
    qkv = (
        jnp.dot(normed, qkv_weight, preferred_element_type=jnp.float32) + qkv_bias
    ).astype(jnp.bfloat16)

    par = parents[:, r, :]
    root = jnp.arange(beams, dtype=jnp.int32)
    roots = []
    for t in range(steps):
        root = root[par[t]]
        roots.append(root)
    roots = jnp.stack(roots, axis=1)
    len_r = lengths[r]
    positions = len_r[roots] + jnp.arange(steps, dtype=jnp.int32)[None, :]

    queries = rotate(qkv[..., :attn_width].reshape(beams, steps, Q_HEADS, head_dim), positions)
    new_keys = rotate(
        qkv[..., attn_width : attn_width + kv_width].reshape(beams, steps, KV_HEADS, head_dim),
        positions,
    )
    new_values = qkv[..., attn_width + kv_width :].reshape(beams, steps, KV_HEADS, head_dim)

    qg = queries.reshape(beams, steps, KV_HEADS, group, head_dim)
    score_parts = []
    for k in range(KV_HEADS):
        keys_k = cache_keys[:, :, k * head_dim : (k + 1) * head_dim]
        score_parts.append(
            jnp.einsum("btgd,cpd->cbtgp", qg[:, :, k], keys_k, preferred_element_type=jnp.float32)
        )
    scores = jnp.stack(score_parts, axis=3) * scale
    my_beams = j * owned + jnp.arange(owned, dtype=jnp.int32)
    limits = len_r[my_beams]
    live = (jnp.arange(context, dtype=jnp.int32)[None, :] < limits[:, None])[
        :, None, None, None, None, :
    ]
    scores = jnp.where(live, scores, masked_score)
    peak = jnp.max(scores, axis=-1)
    weights = jnp.where(live, jnp.exp(scores - peak[..., None]), 0.0)
    total = jnp.sum(weights, axis=-1)
    weights = weights.astype(jnp.bfloat16)
    output = jnp.stack(
        [
            jnp.einsum(
                "cbtgp,cpd->cbtgd",
                weights[:, :, :, k],
                cache_values[:, :, k * head_dim : (k + 1) * head_dim],
                preferred_element_type=jnp.float32,
            )
            for k in range(KV_HEADS)
        ],
        axis=3,
    )
    chosen = (roots[None, :, :] == my_beams[:, None, None])[..., None, None]
    peak = jnp.sum(jnp.where(chosen, peak, 0.0), axis=0)
    total = jnp.sum(jnp.where(chosen, total, 0.0), axis=0)
    output = jnp.sum(jnp.where(chosen[..., None], output, 0.0), axis=0)
    packed = jnp.concatenate([output, peak[..., None], total[..., None]], axis=-1)
    packed = packed.reshape(n_i, owned, steps, KV_HEADS, group, head_dim + 2)
    packed = scatter_rounds(packed, "tpi", j)
    part_output = packed[..., :head_dim]
    part_peak = packed[..., head_dim]
    part_total = packed[..., head_dim + 1]

    anc = []
    for t in range(steps):
        cur = jnp.arange(beams, dtype=jnp.int32)
        row = [None] * steps
        row[t] = cur
        for step in range(t, 0, -1):
            cur = par[step][cur]
            row[step - 1] = cur
        for u in range(t + 1, steps):
            row[u] = jnp.arange(beams, dtype=jnp.int32)
        anc.append(jnp.stack(row, axis=0))
    anc = jnp.stack(anc, axis=0)
    anc_mine = lax.dynamic_slice_in_dim(anc, j * owned, owned, 2)
    anc_mine = jnp.transpose(anc_mine, (2, 0, 1))
    u_index = jnp.broadcast_to(jnp.arange(steps, dtype=jnp.int32), anc_mine.shape)
    hist_keys = new_keys[anc_mine, u_index]
    hist_values = new_values[anc_mine, u_index]
    q_mine = lax.dynamic_slice_in_dim(qg, j * owned, owned, 0)
    recent_scores = jnp.einsum(
        "ctkgd,ctukd->ctkgu", q_mine, hist_keys, preferred_element_type=jnp.float32
    ) * scale
    causal = (
        jnp.arange(steps, dtype=jnp.int32)[None, :] <= jnp.arange(steps, dtype=jnp.int32)[:, None]
    )[None, :, None, None, :]
    recent_scores = jnp.where(causal, recent_scores, masked_score)
    top = jnp.maximum(part_peak, jnp.max(recent_scores, axis=-1))
    factor = jnp.exp(part_peak - top)
    recent_weights = jnp.where(causal, jnp.exp(recent_scores - top[..., None]), 0.0)
    denominator = part_total * factor + jnp.sum(recent_weights, axis=-1)
    numerator = part_output * factor[..., None] + jnp.einsum(
        "ctkgu,ctukd->ctkgd",
        recent_weights.astype(jnp.bfloat16),
        hist_values,
        preferred_element_type=jnp.float32,
    )
    attention = (
        (numerator / denominator[..., None]).reshape(owned, steps, attn_width).astype(jnp.bfloat16)
    )

    att_all = gather_rounds(attention, ALL, flat, flat_masks).reshape(
        requests * beams, steps, attn_width
    )
    my_requests = lax.dynamic_slice_in_dim(slot_request, req_index * group_requests, group_requests)
    att_group = att_all.reshape(requests, beams, steps, attn_width)[my_requests].reshape(
        group_rows, steps, attn_width
    )

    middle = x_group.astype(jnp.float32) + jnp.dot(
        att_group, full_out, preferred_element_type=jnp.float32
    )
    mixed_in = rms_normed(middle)
    gate = jnp.dot(mixed_in, gate_weight, preferred_element_type=jnp.float32)
    upward = jnp.dot(mixed_in, up_weight, preferred_element_type=jnp.float32)
    hidden = (jax.nn.silu(gate) * upward).astype(jnp.bfloat16)
    partial = jnp.dot(hidden, down_weight, preferred_element_type=jnp.float32)
    partial = scatter_rounds(partial.reshape(tp_count, rows_dev * steps, width), TP, tp_index)
    lowered = partial.reshape(rows_dev, steps, width)
    middle_mine = lax.dynamic_slice_in_dim(middle, tp_index * rows_dev, rows_dev, 0)
    result = (middle_mine + lowered).astype(jnp.bfloat16)
    return jnp.swapaxes(result, 0, 1)


def solution(mesh):
    n_req = mesh.shape["req"]
    n_tp = mesh.shape["tp"]
    inner = 4
    devices = mesh.devices.reshape(n_req, n_tp // inner, inner)
    sub = Mesh(devices, ALL)
    rows = P(None, ALL, None)
    in_specs = (
        rows,
        P(),
        P(),
        P(TP, None),
        P(None, TP),
        P(None, TP),
        P(TP, None),
        P(ALL, None, None),
        P(ALL, None, None),
        P(),
        P(),
        P(),
    )
    return jax.shard_map(per_device, mesh=sub, in_specs=in_specs, out_specs=rows, check_vma=False)
```

```python
import jax
import jax.numpy as jnp
from jax import lax
import functools

from jax.experimental import pallas as pl
from jax.experimental.pallas import tpu as pltpu
from jax.sharding import Mesh
from jax.sharding import PartitionSpec as P

Q_HEADS = 12
KV_HEADS = 2

theta_base = 1000000.0
norm_eps = 1e-06
masked_score = -1e30

ALL = ("req", "tpo", "tpi")
TP = ("tpo", "tpi")


def rms_normed(values):
    values = values.astype(jnp.float32)
    factor = lax.rsqrt(jnp.mean(values * values, axis=-1, keepdims=True) + norm_eps)
    return (values * factor).astype(jnp.bfloat16)


def rotate(vectors, positions):
    half = vectors.shape[-1] // 2
    freqs = theta_base ** (-jnp.arange(half, dtype=jnp.float32) * 2.0 / vectors.shape[-1])
    angles = positions.astype(jnp.float32)[..., None] * freqs
    cosine = jnp.cos(angles)[..., None, :]
    sine = jnp.sin(angles)[..., None, :]
    values = vectors.astype(jnp.float32)
    first = values[..., :half]
    second = values[..., half:]
    return jnp.concatenate(
        [first * cosine - second * sine, second * cosine + first * sine], axis=-1
    ).astype(jnp.bfloat16)


def _prefix_kernel(limits_ref, q_ref, k_ref, v_ref, o_ref, m_ref, l_ref, *, scale, masked):
    c = pl.program_id(0)
    q = q_ref[0]
    keys = k_ref[0]
    s = lax.dot_general(q, keys, (((1,), (1,)), ((), ())), preferred_element_type=jnp.float32) * scale
    col = lax.broadcasted_iota(jnp.int32, s.shape, 1)
    live = col < limits_ref[c]
    s = jnp.where(live, s, masked)
    m = jnp.max(s, axis=1, keepdims=True)
    w = jnp.where(live, jnp.exp(s - m), 0.0)
    l = jnp.sum(w, axis=1, keepdims=True)
    o = jnp.dot(w.astype(jnp.bfloat16), v_ref[0], preferred_element_type=jnp.float32)
    o_ref[0, 0] = o
    m_ref[0, 0] = m
    l_ref[0, 0] = l


def prefix_attention(q, keys, values, limits, scale, masked, interpret=False):
    kvh, rows, d = q.shape
    cache_rows, ctx, _ = keys.shape
    kern = functools.partial(_prefix_kernel, scale=scale, masked=masked)
    return pl.pallas_call(
        kern,
        out_shape=(
            jax.ShapeDtypeStruct((cache_rows, kvh, rows, d), jnp.float32),
            jax.ShapeDtypeStruct((cache_rows, kvh, rows, 1), jnp.float32),
            jax.ShapeDtypeStruct((cache_rows, kvh, rows, 1), jnp.float32),
        ),
        grid_spec=pltpu.PrefetchScalarGridSpec(
            num_scalar_prefetch=1,
            grid=(cache_rows, kvh),
            in_specs=[
                pl.BlockSpec((1, rows, d), lambda c, k, lim: (k, 0, 0)),
                pl.BlockSpec((1, ctx, d), lambda c, k, lim: (c, 0, k)),
                pl.BlockSpec((1, ctx, d), lambda c, k, lim: (c, 0, k)),
            ],
            out_specs=[
                pl.BlockSpec((1, 1, rows, d), lambda c, k, lim: (c, k, 0, 0)),
                pl.BlockSpec((1, 1, rows, 1), lambda c, k, lim: (c, k, 0, 0)),
                pl.BlockSpec((1, 1, rows, 1), lambda c, k, lim: (c, k, 0, 0)),
            ],
        ),
        interpret=interpret,
    )(limits, q, keys, values)


def gather_rounds(x, axes, index, masks):
    count = 1 << len(masks)
    buf = x
    bits = []
    for mask in masks:
        low = mask & (-mask)
        bit = low if mask == low else mask - low
        perm = [(i, i ^ mask) for i in range(count)]
        recv = lax.ppermute(buf, axes, perm)
        mine = (index // bit) % 2
        buf = jnp.where(mine == 0, jnp.stack([buf, recv]), jnp.stack([recv, buf]))
        bits.append(bit)
    depth = len(bits)
    order = sorted(range(depth), key=lambda a: -bits[depth - 1 - a])
    buf = jnp.transpose(buf, tuple(order) + tuple(range(depth, buf.ndim)))
    return buf.reshape((count,) + x.shape)


def scatter_rounds(x, axes, index):
    count = x.shape[0]
    buf = x
    bit = 1
    while bit < count:
        pairs = buf.reshape((buf.shape[0] // 2, 2) + buf.shape[1:])
        mine = (index // bit) % 2
        keep = jnp.where(mine == 0, pairs[:, 0], pairs[:, 1])
        send = jnp.where(mine == 0, pairs[:, 1], pairs[:, 0])
        perm = [(i, i ^ bit) for i in range(count)]
        buf = keep + lax.ppermute(send, axes, perm)
        bit *= 2
    return buf[0]


def gather_masks(n_req, tp_count):
    masks = []
    for shift, size in ((tp_count.bit_length() - 1, n_req), (3, 4), (1, 4)):
        low = 1 << shift
        masks.append(low)
        if size == 4:
            masks.append(3 * low)
    masks.append(1)
    return masks


def per_device(
    step_inputs,
    qkv_weight,
    qkv_bias,
    out_weight,
    gate_weight,
    up_weight,
    down_weight,
    cache_keys,
    cache_values,
    lengths,
    parents,
    slot_request,
):
    steps, rows_dev, width = step_inputs.shape
    beams = parents.shape[2]
    requests = slot_request.shape[0]
    n_req = lax.axis_size("req")
    n_o = lax.axis_size("tpo")
    n_i = lax.axis_size("tpi")
    tp_count = n_o * n_i
    group_requests = requests // n_req
    group_rows = group_requests * beams
    owned, context, kv_width = cache_keys.shape
    head_dim = kv_width // KV_HEADS
    group = Q_HEADS // KV_HEADS
    attn_width = Q_HEADS * head_dim
    scale = head_dim ** (-0.5)
    assert owned * n_i == beams

    req_index = lax.axis_index("req")
    tp_index = lax.axis_index("tpo") * n_i + lax.axis_index("tpi")
    j = lax.axis_index("tpi")
    flat = req_index * tp_count + tp_index
    r = flat // n_i

    inverse = (
        jnp.zeros((requests,), jnp.int32)
        .at[slot_request]
        .set(jnp.arange(requests, dtype=jnp.int32))
    )

    flat_masks = gather_masks(n_req, tp_count)
    x_all = gather_rounds(
        jnp.swapaxes(step_inputs, 0, 1).reshape(rows_dev * steps, width), ALL, flat, flat_masks
    ).reshape(requests * beams, steps, width)
    after_rows = (x_all[0, 0, 0] * 0).astype(out_weight.dtype)
    full_out = lax.all_gather(out_weight + after_rows, TP, axis=0, tiled=True)
    x_req = lax.dynamic_slice_in_dim(x_all, inverse[r] * beams, beams, 0)
    x_group = lax.dynamic_slice_in_dim(x_all, req_index * group_rows, group_rows, 0)

    normed = rms_normed(x_req)
    qkv = (
        jnp.dot(normed, qkv_weight, preferred_element_type=jnp.float32) + qkv_bias
    ).astype(jnp.bfloat16)

    par = parents[:, r, :]
    root = jnp.arange(beams, dtype=jnp.int32)
    roots = []
    for t in range(steps):
        root = root[par[t]]
        roots.append(root)
    roots = jnp.stack(roots, axis=1)
    len_r = lengths[r]
    positions = len_r[roots] + jnp.arange(steps, dtype=jnp.int32)[None, :]

    queries = rotate(qkv[..., :attn_width].reshape(beams, steps, Q_HEADS, head_dim), positions)
    new_keys = rotate(
        qkv[..., attn_width : attn_width + kv_width].reshape(beams, steps, KV_HEADS, head_dim),
        positions,
    )
    new_values = qkv[..., attn_width + kv_width :].reshape(beams, steps, KV_HEADS, head_dim)

    qg = queries.reshape(beams, steps, KV_HEADS, group, head_dim)
    my_beams = j * owned + jnp.arange(owned, dtype=jnp.int32)
    limits = len_r[my_beams]
    q_heads = jnp.transpose(qg, (2, 0, 1, 3, 4)).reshape(KV_HEADS, beams * steps * group, head_dim)
    output, peak, total = prefix_attention(
        q_heads, cache_keys, cache_values, limits, scale, masked_score
    )
    output = output.reshape(owned, KV_HEADS, beams, steps, group, head_dim).transpose(0, 2, 3, 1, 4, 5)
    peak = peak.reshape(owned, KV_HEADS, beams, steps, group).transpose(0, 2, 3, 1, 4)
    total = total.reshape(owned, KV_HEADS, beams, steps, group).transpose(0, 2, 3, 1, 4)
    chosen = (roots[None, :, :] == my_beams[:, None, None])[..., None, None]
    peak = jnp.sum(jnp.where(chosen, peak, 0.0), axis=0)
    total = jnp.sum(jnp.where(chosen, total, 0.0), axis=0)
    output = jnp.sum(jnp.where(chosen[..., None], output, 0.0), axis=0)
    packed = jnp.concatenate([output, peak[..., None], total[..., None]], axis=-1)
    packed = packed.reshape(n_i, owned, steps, KV_HEADS, group, head_dim + 2)
    packed = scatter_rounds(packed, "tpi", j)
    part_output = packed[..., :head_dim]
    part_peak = packed[..., head_dim]
    part_total = packed[..., head_dim + 1]

    anc = []
    for t in range(steps):
        cur = jnp.arange(beams, dtype=jnp.int32)
        row = [None] * steps
        row[t] = cur
        for step in range(t, 0, -1):
            cur = par[step][cur]
            row[step - 1] = cur
        for u in range(t + 1, steps):
            row[u] = jnp.arange(beams, dtype=jnp.int32)
        anc.append(jnp.stack(row, axis=0))
    anc = jnp.stack(anc, axis=0)
    anc_mine = lax.dynamic_slice_in_dim(anc, j * owned, owned, 2)
    anc_mine = jnp.transpose(anc_mine, (2, 0, 1))
    u_index = jnp.broadcast_to(jnp.arange(steps, dtype=jnp.int32), anc_mine.shape)
    hist_keys = new_keys[anc_mine, u_index]
    hist_values = new_values[anc_mine, u_index]
    q_mine = lax.dynamic_slice_in_dim(qg, j * owned, owned, 0)
    recent_scores = jnp.einsum(
        "ctkgd,ctukd->ctkgu", q_mine, hist_keys, preferred_element_type=jnp.float32
    ) * scale
    causal = (
        jnp.arange(steps, dtype=jnp.int32)[None, :] <= jnp.arange(steps, dtype=jnp.int32)[:, None]
    )[None, :, None, None, :]
    recent_scores = jnp.where(causal, recent_scores, masked_score)
    top = jnp.maximum(part_peak, jnp.max(recent_scores, axis=-1))
    factor = jnp.exp(part_peak - top)
    recent_weights = jnp.where(causal, jnp.exp(recent_scores - top[..., None]), 0.0)
    denominator = part_total * factor + jnp.sum(recent_weights, axis=-1)
    numerator = part_output * factor[..., None] + jnp.einsum(
        "ctkgu,ctukd->ctkgd",
        recent_weights.astype(jnp.bfloat16),
        hist_values,
        preferred_element_type=jnp.float32,
    )
    attention = (
        (numerator / denominator[..., None]).reshape(owned, steps, attn_width).astype(jnp.bfloat16)
    )

    att_all = gather_rounds(attention, ALL, flat, flat_masks).reshape(
        requests * beams, steps, attn_width
    )
    my_requests = lax.dynamic_slice_in_dim(slot_request, req_index * group_requests, group_requests)
    att_group = att_all.reshape(requests, beams, steps, attn_width)[my_requests].reshape(
        group_rows, steps, attn_width
    )

    middle = x_group.astype(jnp.float32) + jnp.dot(
        att_group, full_out, preferred_element_type=jnp.float32
    )
    mixed_in = rms_normed(middle)
    gate = jnp.dot(mixed_in, gate_weight, preferred_element_type=jnp.float32)
    upward = jnp.dot(mixed_in, up_weight, preferred_element_type=jnp.float32)
    hidden = (jax.nn.silu(gate) * upward).astype(jnp.bfloat16)
    partial = jnp.dot(hidden, down_weight, preferred_element_type=jnp.float32)
    partial = scatter_rounds(partial.reshape(tp_count, rows_dev * steps, width), TP, tp_index)
    lowered = partial.reshape(rows_dev, steps, width)
    middle_mine = lax.dynamic_slice_in_dim(middle, tp_index * rows_dev, rows_dev, 0)
    result = (middle_mine + lowered).astype(jnp.bfloat16)
    return jnp.swapaxes(result, 0, 1)


def solution(mesh):
    n_req = mesh.shape["req"]
    n_tp = mesh.shape["tp"]
    inner = 4
    devices = mesh.devices.reshape(n_req, n_tp // inner, inner)
    sub = Mesh(devices, ALL)
    rows = P(None, ALL, None)
    in_specs = (
        rows,
        P(),
        P(),
        P(TP, None),
        P(None, TP),
        P(None, TP),
        P(TP, None),
        P(ALL, None, None),
        P(ALL, None, None),
        P(),
        P(),
        P(),
    )
    return jax.shard_map(per_device, mesh=sub, in_specs=in_specs, out_specs=rows, check_vma=False)
```

```python
import jax
import jax.numpy as jnp
from jax import lax
from jax.sharding import Mesh
from jax.sharding import PartitionSpec as P

Q_HEADS = 12
KV_HEADS = 2

theta_base = 1000000.0
norm_eps = 1e-06
masked_score = -1e30

ALL = ("req", "tpo", "tpi")
TP = ("tpo", "tpi")


def rms_normed(values):
    values = values.astype(jnp.float32)
    factor = lax.rsqrt(jnp.mean(values * values, axis=-1, keepdims=True) + norm_eps)
    return (values * factor).astype(jnp.bfloat16)


def rotate(vectors, positions):
    half = vectors.shape[-1] // 2
    freqs = theta_base ** (-jnp.arange(half, dtype=jnp.float32) * 2.0 / vectors.shape[-1])
    angles = positions.astype(jnp.float32)[..., None] * freqs
    cosine = jnp.cos(angles)[..., None, :]
    sine = jnp.sin(angles)[..., None, :]
    values = vectors.astype(jnp.float32)
    first = values[..., :half]
    second = values[..., half:]
    return jnp.concatenate(
        [first * cosine - second * sine, second * cosine + first * sine], axis=-1
    ).astype(jnp.bfloat16)


def gather_rounds(x, axes, index, masks):
    count = 1 << len(masks)
    buf = x
    bits = []
    for mask in masks:
        low = mask & (-mask)
        bit = low if mask == low else mask - low
        perm = [(i, i ^ mask) for i in range(count)]
        recv = lax.ppermute(buf, axes, perm)
        mine = (index // bit) % 2
        buf = jnp.where(mine == 0, jnp.stack([buf, recv]), jnp.stack([recv, buf]))
        bits.append(bit)
    depth = len(bits)
    flat_buf = buf.reshape((count,) + x.shape)

    def position(device):
        pos = jnp.zeros_like(device)
        for a in range(depth):
            pos = pos + ((device // bits[depth - 1 - a]) % 2) * (1 << (depth - 1 - a))
        return pos

    return flat_buf, position


def scatter_rounds(x, axes, index):
    count = x.shape[0]
    buf = x
    bit = 1
    while bit < count:
        pairs = buf.reshape((buf.shape[0] // 2, 2) + buf.shape[1:])
        mine = (index // bit) % 2
        keep = jnp.where(mine == 0, pairs[:, 0], pairs[:, 1])
        send = jnp.where(mine == 0, pairs[:, 1], pairs[:, 0])
        perm = [(i, i ^ bit) for i in range(count)]
        buf = keep + lax.ppermute(send, axes, perm)
        bit *= 2
    return buf[0]


def gather_masks(n_req, tp_count):
    masks = []
    for shift, size in ((tp_count.bit_length() - 1, n_req), (3, 4), (1, 4)):
        low = 1 << shift
        masks.append(low)
        if size == 4:
            masks.append(3 * low)
    masks.append(1)
    return masks


def per_device(
    step_inputs,
    qkv_weight,
    qkv_bias,
    out_weight,
    gate_weight,
    up_weight,
    down_weight,
    cache_keys,
    cache_values,
    lengths,
    parents,
    slot_request,
):
    steps, rows_dev, width = step_inputs.shape
    beams = parents.shape[2]
    requests = slot_request.shape[0]
    n_req = lax.axis_size("req")
    n_o = lax.axis_size("tpo")
    n_i = lax.axis_size("tpi")
    tp_count = n_o * n_i
    group_requests = requests // n_req
    group_rows = group_requests * beams
    owned, context, kv_width = cache_keys.shape
    head_dim = kv_width // KV_HEADS
    group = Q_HEADS // KV_HEADS
    attn_width = Q_HEADS * head_dim
    scale = head_dim ** (-0.5)
    assert owned * n_i == beams

    req_index = lax.axis_index("req")
    tp_index = lax.axis_index("tpo") * n_i + lax.axis_index("tpi")
    j = lax.axis_index("tpi")
    flat = req_index * tp_count + tp_index
    r = flat // n_i

    inverse = (
        jnp.zeros((requests,), jnp.int32)
        .at[slot_request]
        .set(jnp.arange(requests, dtype=jnp.int32))
    )

    flat_masks = gather_masks(n_req, tp_count)
    x_blocks, x_position = gather_rounds(
        jnp.swapaxes(step_inputs, 0, 1).reshape(rows_dev * steps, width), ALL, flat, flat_masks
    )
    x_blocks = x_blocks.reshape(x_blocks.shape[0], rows_dev, steps, width)
    slot_devices = inverse[r] * n_i + jnp.arange(n_i, dtype=jnp.int32)
    x_req = x_blocks[x_position(slot_devices)].reshape(beams, steps, width)
    group_devices = req_index * tp_count + jnp.arange(tp_count, dtype=jnp.int32)
    x_group = x_blocks[x_position(group_devices)].reshape(group_rows, steps, width)
    after_rows = (x_blocks[0, 0, 0, 0] * 0).astype(out_weight.dtype)
    full_out = lax.all_gather(out_weight + after_rows, TP, axis=0, tiled=True)

    normed = rms_normed(x_req)
    qkv = (
        jnp.dot(normed, qkv_weight, preferred_element_type=jnp.float32) + qkv_bias
    ).astype(jnp.bfloat16)

    par = parents[:, r, :]
    root = jnp.arange(beams, dtype=jnp.int32)
    roots = []
    for t in range(steps):
        root = root[par[t]]
        roots.append(root)
    roots = jnp.stack(roots, axis=1)
    len_r = lengths[r]
    positions = len_r[roots] + jnp.arange(steps, dtype=jnp.int32)[None, :]

    queries = rotate(qkv[..., :attn_width].reshape(beams, steps, Q_HEADS, head_dim), positions)
    new_keys = rotate(
        qkv[..., attn_width : attn_width + kv_width].reshape(beams, steps, KV_HEADS, head_dim),
        positions,
    )
    new_values = qkv[..., attn_width + kv_width :].reshape(beams, steps, KV_HEADS, head_dim)

    qg = queries.reshape(beams, steps, KV_HEADS, group, head_dim)
    score_parts = []
    for k in range(KV_HEADS):
        keys_k = cache_keys[:, :, k * head_dim : (k + 1) * head_dim]
        score_parts.append(
            jnp.einsum("btgd,cpd->cbtgp", qg[:, :, k], keys_k, preferred_element_type=jnp.float32)
        )
    scores = jnp.stack(score_parts, axis=3) * scale
    my_beams = j * owned + jnp.arange(owned, dtype=jnp.int32)
    limits = len_r[my_beams]
    live = (jnp.arange(context, dtype=jnp.int32)[None, :] < limits[:, None])[
        :, None, None, None, None, :
    ]
    scores = jnp.where(live, scores, masked_score)
    peak = jnp.max(scores, axis=-1)
    weights = jnp.where(live, jnp.exp(scores - peak[..., None]), 0.0)
    total = jnp.sum(weights, axis=-1)
    weights = weights.astype(jnp.bfloat16)
    output = jnp.stack(
        [
            jnp.einsum(
                "cbtgp,cpd->cbtgd",
                weights[:, :, :, k],
                cache_values[:, :, k * head_dim : (k + 1) * head_dim],
                preferred_element_type=jnp.float32,
            )
            for k in range(KV_HEADS)
        ],
        axis=3,
    )
    chosen = (roots[None, :, :] == my_beams[:, None, None])[..., None, None]
    peak = jnp.sum(jnp.where(chosen, peak, 0.0), axis=0)
    total = jnp.sum(jnp.where(chosen, total, 0.0), axis=0)
    output = jnp.sum(jnp.where(chosen[..., None], output, 0.0), axis=0)
    packed = jnp.concatenate([output, peak[..., None], total[..., None]], axis=-1)
    packed = packed.reshape(n_i, owned, steps, KV_HEADS, group, head_dim + 2)
    packed = scatter_rounds(packed, "tpi", j)
    part_output = packed[..., :head_dim]
    part_peak = packed[..., head_dim]
    part_total = packed[..., head_dim + 1]

    anc = []
    for t in range(steps):
        cur = jnp.arange(beams, dtype=jnp.int32)
        row = [None] * steps
        row[t] = cur
        for step in range(t, 0, -1):
            cur = par[step][cur]
            row[step - 1] = cur
        for u in range(t + 1, steps):
            row[u] = jnp.arange(beams, dtype=jnp.int32)
        anc.append(jnp.stack(row, axis=0))
    anc = jnp.stack(anc, axis=0)
    anc_mine = lax.dynamic_slice_in_dim(anc, j * owned, owned, 2)
    anc_mine = jnp.transpose(anc_mine, (2, 0, 1))
    u_index = jnp.broadcast_to(jnp.arange(steps, dtype=jnp.int32), anc_mine.shape)
    hist_keys = new_keys[anc_mine, u_index]
    hist_values = new_values[anc_mine, u_index]
    q_mine = lax.dynamic_slice_in_dim(qg, j * owned, owned, 0)
    recent_scores = jnp.einsum(
        "ctkgd,ctukd->ctkgu", q_mine, hist_keys, preferred_element_type=jnp.float32
    ) * scale
    causal = (
        jnp.arange(steps, dtype=jnp.int32)[None, :] <= jnp.arange(steps, dtype=jnp.int32)[:, None]
    )[None, :, None, None, :]
    recent_scores = jnp.where(causal, recent_scores, masked_score)
    top = jnp.maximum(part_peak, jnp.max(recent_scores, axis=-1))
    factor = jnp.exp(part_peak - top)
    recent_weights = jnp.where(causal, jnp.exp(recent_scores - top[..., None]), 0.0)
    denominator = part_total * factor + jnp.sum(recent_weights, axis=-1)
    numerator = part_output * factor[..., None] + jnp.einsum(
        "ctkgu,ctukd->ctkgd",
        recent_weights.astype(jnp.bfloat16),
        hist_values,
        preferred_element_type=jnp.float32,
    )
    attention = (
        (numerator / denominator[..., None]).reshape(owned, steps, attn_width).astype(jnp.bfloat16)
    )

    att_blocks, att_position = gather_rounds(attention, ALL, flat, flat_masks)
    my_requests = lax.dynamic_slice_in_dim(slot_request, req_index * group_requests, group_requests)
    owner_devices = (my_requests[:, None] * n_i + jnp.arange(n_i, dtype=jnp.int32)[None, :]).reshape(-1)
    att_group = att_blocks[att_position(owner_devices)].reshape(group_rows, steps, attn_width)

    middle = x_group.astype(jnp.float32) + jnp.dot(
        att_group, full_out, preferred_element_type=jnp.float32
    )
    mixed_in = rms_normed(middle)
    gate = jnp.dot(mixed_in, gate_weight, preferred_element_type=jnp.float32)
    upward = jnp.dot(mixed_in, up_weight, preferred_element_type=jnp.float32)
    hidden = (jax.nn.silu(gate) * upward).astype(jnp.bfloat16)
    partial = jnp.dot(hidden, down_weight, preferred_element_type=jnp.float32)
    partial = scatter_rounds(partial.reshape(tp_count, rows_dev * steps, width), TP, tp_index)
    lowered = partial.reshape(rows_dev, steps, width)
    middle_mine = lax.dynamic_slice_in_dim(middle, tp_index * rows_dev, rows_dev, 0)
    result = (middle_mine + lowered).astype(jnp.bfloat16)
    return jnp.swapaxes(result, 0, 1)


def solution(mesh):
    n_req = mesh.shape["req"]
    n_tp = mesh.shape["tp"]
    inner = 4
    devices = mesh.devices.reshape(n_req, n_tp // inner, inner)
    sub = Mesh(devices, ALL)
    rows = P(None, ALL, None)
    in_specs = (
        rows,
        P(),
        P(),
        P(TP, None),
        P(None, TP),
        P(None, TP),
        P(TP, None),
        P(ALL, None, None),
        P(ALL, None, None),
        P(),
        P(),
        P(),
    )
    return jax.shard_map(per_device, mesh=sub, in_specs=in_specs, out_specs=rows, check_vma=False)
```

```python
import jax
import jax.numpy as jnp
from jax import lax
from jax.sharding import Mesh
from jax.sharding import PartitionSpec as P

Q_HEADS = 12
KV_HEADS = 2

theta_base = 1000000.0
norm_eps = 1e-06
masked_score = -1e30

ALL = ("req", "tpo", "tpi")
TP = ("tpo", "tpi")


def rms_normed(values):
    values = values.astype(jnp.float32)
    factor = lax.rsqrt(jnp.mean(values * values, axis=-1, keepdims=True) + norm_eps)
    return (values * factor).astype(jnp.bfloat16)


def rotate(vectors, positions):
    half = vectors.shape[-1] // 2
    freqs = theta_base ** (-jnp.arange(half, dtype=jnp.float32) * 2.0 / vectors.shape[-1])
    angles = positions.astype(jnp.float32)[..., None] * freqs
    cosine = jnp.cos(angles)[..., None, :]
    sine = jnp.sin(angles)[..., None, :]
    values = vectors.astype(jnp.float32)
    first = values[..., :half]
    second = values[..., half:]
    return jnp.concatenate(
        [first * cosine - second * sine, second * cosine + first * sine], axis=-1
    ).astype(jnp.bfloat16)


def gather_rounds(x, axes, index, masks):
    count = 1 << len(masks)
    buf = x
    bits = []
    for mask in masks:
        low = mask & (-mask)
        bit = low if mask == low else mask - low
        perm = [(i, i ^ mask) for i in range(count)]
        recv = lax.ppermute(buf, axes, perm)
        if mask != low:
            recv = jnp.flip(recv, axis=0)
        buf = jnp.stack([buf, recv])
        bits.append(bit)
    depth = len(bits)
    flat_buf = buf.reshape((count,) + x.shape)

    def position(device):
        pos = jnp.zeros_like(device)
        for a in range(depth):
            bit = bits[depth - 1 - a]
            slot = ((device // bit) % 2) ^ ((index // bit) % 2)
            pos = pos + slot * (1 << (depth - 1 - a))
        return pos

    return flat_buf, position


def scatter_rounds(x, axes, index):
    count = x.shape[0]
    buf = x
    bit = 1
    while bit < count:
        pairs = buf.reshape((buf.shape[0] // 2, 2) + buf.shape[1:])
        mine = (index // bit) % 2
        keep = jnp.where(mine == 0, pairs[:, 0], pairs[:, 1])
        send = jnp.where(mine == 0, pairs[:, 1], pairs[:, 0])
        perm = [(i, i ^ bit) for i in range(count)]
        buf = keep + lax.ppermute(send, axes, perm)
        bit *= 2
    return buf[0]


def gather_masks(n_req, tp_count):
    masks = []
    for shift, size in ((tp_count.bit_length() - 1, n_req), (3, 4), (1, 4)):
        low = 1 << shift
        masks.append(low)
        if size == 4:
            masks.append(3 * low)
    masks.append(1)
    return masks


def per_device(
    step_inputs,
    qkv_weight,
    qkv_bias,
    out_weight,
    gate_weight,
    up_weight,
    down_weight,
    cache_keys,
    cache_values,
    lengths,
    parents,
    slot_request,
):
    steps, rows_dev, width = step_inputs.shape
    beams = parents.shape[2]
    requests = slot_request.shape[0]
    n_req = lax.axis_size("req")
    n_o = lax.axis_size("tpo")
    n_i = lax.axis_size("tpi")
    tp_count = n_o * n_i
    group_requests = requests // n_req
    group_rows = group_requests * beams
    owned, context, kv_width = cache_keys.shape
    head_dim = kv_width // KV_HEADS
    group = Q_HEADS // KV_HEADS
    attn_width = Q_HEADS * head_dim
    scale = head_dim ** (-0.5)
    assert owned * n_i == beams

    req_index = lax.axis_index("req")
    tp_index = lax.axis_index("tpo") * n_i + lax.axis_index("tpi")
    j = lax.axis_index("tpi")
    flat = req_index * tp_count + tp_index
    r = flat // n_i

    inverse = (
        jnp.zeros((requests,), jnp.int32)
        .at[slot_request]
        .set(jnp.arange(requests, dtype=jnp.int32))
    )

    flat_masks = gather_masks(n_req, tp_count)
    x_blocks, x_position = gather_rounds(
        jnp.swapaxes(step_inputs, 0, 1).reshape(rows_dev * steps, width), ALL, flat, flat_masks
    )
    x_blocks = x_blocks.reshape(x_blocks.shape[0], rows_dev, steps, width)
    slot_devices = inverse[r] * n_i + jnp.arange(n_i, dtype=jnp.int32)
    x_req = x_blocks[x_position(slot_devices)].reshape(beams, steps, width)
    group_devices = req_index * tp_count + jnp.arange(tp_count, dtype=jnp.int32)
    x_group = x_blocks[x_position(group_devices)].reshape(group_rows, steps, width)
    after_rows = (x_blocks[0, 0, 0, 0] * 0).astype(out_weight.dtype)
    full_out = lax.all_gather(out_weight + after_rows, TP, axis=0, tiled=True)

    normed = rms_normed(x_req)
    qkv = (
        jnp.dot(normed, qkv_weight, preferred_element_type=jnp.float32) + qkv_bias
    ).astype(jnp.bfloat16)

    par = parents[:, r, :]
    root = jnp.arange(beams, dtype=jnp.int32)
    roots = []
    for t in range(steps):
        root = root[par[t]]
        roots.append(root)
    roots = jnp.stack(roots, axis=1)
    len_r = lengths[r]
    positions = len_r[roots] + jnp.arange(steps, dtype=jnp.int32)[None, :]

    queries = rotate(qkv[..., :attn_width].reshape(beams, steps, Q_HEADS, head_dim), positions)
    new_keys = rotate(
        qkv[..., attn_width : attn_width + kv_width].reshape(beams, steps, KV_HEADS, head_dim),
        positions,
    )
    new_values = qkv[..., attn_width + kv_width :].reshape(beams, steps, KV_HEADS, head_dim)

    qg = queries.reshape(beams, steps, KV_HEADS, group, head_dim)
    score_parts = []
    for k in range(KV_HEADS):
        keys_k = cache_keys[:, :, k * head_dim : (k + 1) * head_dim]
        score_parts.append(
            jnp.einsum("btgd,cpd->cbtgp", qg[:, :, k], keys_k, preferred_element_type=jnp.float32)
        )
    scores = jnp.stack(score_parts, axis=3) * scale
    my_beams = j * owned + jnp.arange(owned, dtype=jnp.int32)
    limits = len_r[my_beams]
    live = (jnp.arange(context, dtype=jnp.int32)[None, :] < limits[:, None])[
        :, None, None, None, None, :
    ]
    scores = jnp.where(live, scores, masked_score)
    peak = jnp.max(scores, axis=-1)
    weights = jnp.where(live, jnp.exp(scores - peak[..., None]), 0.0)
    total = jnp.sum(weights, axis=-1)
    weights = weights.astype(jnp.bfloat16)
    output = jnp.stack(
        [
            jnp.einsum(
                "cbtgp,cpd->cbtgd",
                weights[:, :, :, k],
                cache_values[:, :, k * head_dim : (k + 1) * head_dim],
                preferred_element_type=jnp.float32,
            )
            for k in range(KV_HEADS)
        ],
        axis=3,
    )
    chosen = (roots[None, :, :] == my_beams[:, None, None])[..., None, None]
    peak = jnp.sum(jnp.where(chosen, peak, 0.0), axis=0)
    total = jnp.sum(jnp.where(chosen, total, 0.0), axis=0)
    output = jnp.sum(jnp.where(chosen[..., None], output, 0.0), axis=0)
    packed = jnp.concatenate([output, peak[..., None], total[..., None]], axis=-1)
    packed = packed.reshape(n_i, owned, steps, KV_HEADS, group, head_dim + 2)
    packed = scatter_rounds(packed, "tpi", j)
    part_output = packed[..., :head_dim]
    part_peak = packed[..., head_dim]
    part_total = packed[..., head_dim + 1]

    anc = []
    for t in range(steps):
        cur = jnp.arange(beams, dtype=jnp.int32)
        row = [None] * steps
        row[t] = cur
        for step in range(t, 0, -1):
            cur = par[step][cur]
            row[step - 1] = cur
        for u in range(t + 1, steps):
            row[u] = jnp.arange(beams, dtype=jnp.int32)
        anc.append(jnp.stack(row, axis=0))
    anc = jnp.stack(anc, axis=0)
    anc_mine = lax.dynamic_slice_in_dim(anc, j * owned, owned, 2)
    anc_mine = jnp.transpose(anc_mine, (2, 0, 1))
    u_index = jnp.broadcast_to(jnp.arange(steps, dtype=jnp.int32), anc_mine.shape)
    hist_keys = new_keys[anc_mine, u_index]
    hist_values = new_values[anc_mine, u_index]
    q_mine = lax.dynamic_slice_in_dim(qg, j * owned, owned, 0)
    recent_scores = jnp.einsum(
        "ctkgd,ctukd->ctkgu", q_mine, hist_keys, preferred_element_type=jnp.float32
    ) * scale
    causal = (
        jnp.arange(steps, dtype=jnp.int32)[None, :] <= jnp.arange(steps, dtype=jnp.int32)[:, None]
    )[None, :, None, None, :]
    recent_scores = jnp.where(causal, recent_scores, masked_score)
    top = jnp.maximum(part_peak, jnp.max(recent_scores, axis=-1))
    factor = jnp.exp(part_peak - top)
    recent_weights = jnp.where(causal, jnp.exp(recent_scores - top[..., None]), 0.0)
    denominator = part_total * factor + jnp.sum(recent_weights, axis=-1)
    numerator = part_output * factor[..., None] + jnp.einsum(
        "ctkgu,ctukd->ctkgd",
        recent_weights.astype(jnp.bfloat16),
        hist_values,
        preferred_element_type=jnp.float32,
    )
    attention = (
        (numerator / denominator[..., None]).reshape(owned, steps, attn_width).astype(jnp.bfloat16)
    )

    att_blocks, att_position = gather_rounds(attention, ALL, flat, flat_masks)
    my_requests = lax.dynamic_slice_in_dim(slot_request, req_index * group_requests, group_requests)
    owner_devices = (my_requests[:, None] * n_i + jnp.arange(n_i, dtype=jnp.int32)[None, :]).reshape(-1)
    att_group = att_blocks[att_position(owner_devices)].reshape(group_rows, steps, attn_width)

    middle = x_group.astype(jnp.float32) + jnp.dot(
        att_group, full_out, preferred_element_type=jnp.float32
    )
    mixed_in = rms_normed(middle)
    gate = jnp.dot(mixed_in, gate_weight, preferred_element_type=jnp.float32)
    upward = jnp.dot(mixed_in, up_weight, preferred_element_type=jnp.float32)
    hidden = (jax.nn.silu(gate) * upward).astype(jnp.bfloat16)
    partial = jnp.dot(hidden, down_weight, preferred_element_type=jnp.float32)
    partial = scatter_rounds(partial.reshape(tp_count, rows_dev * steps, width), TP, tp_index)
    lowered = partial.reshape(rows_dev, steps, width)
    middle_mine = lax.dynamic_slice_in_dim(middle, tp_index * rows_dev, rows_dev, 0)
    result = (middle_mine + lowered).astype(jnp.bfloat16)
    return jnp.swapaxes(result, 0, 1)


def solution(mesh):
    n_req = mesh.shape["req"]
    n_tp = mesh.shape["tp"]
    inner = 4
    devices = mesh.devices.reshape(n_req, n_tp // inner, inner)
    sub = Mesh(devices, ALL)
    rows = P(None, ALL, None)
    in_specs = (
        rows,
        P(),
        P(),
        P(TP, None),
        P(None, TP),
        P(None, TP),
        P(TP, None),
        P(ALL, None, None),
        P(ALL, None, None),
        P(),
        P(),
        P(),
    )
    return jax.shard_map(per_device, mesh=sub, in_specs=in_specs, out_specs=rows, check_vma=False)
```

```python
import jax
import jax.numpy as jnp
from jax import lax
from jax.sharding import Mesh
from jax.sharding import PartitionSpec as P

Q_HEADS = 12
KV_HEADS = 2

theta_base = 1000000.0
norm_eps = 1e-06
masked_score = -1e30

ALL = ("req", "tpo", "tpi")
TP = ("tpo", "tpi")


def rms_normed(values):
    values = values.astype(jnp.float32)
    factor = lax.rsqrt(jnp.mean(values * values, axis=-1, keepdims=True) + norm_eps)
    return (values * factor).astype(jnp.bfloat16)


def rotate(vectors, positions):
    half = vectors.shape[-1] // 2
    freqs = theta_base ** (-jnp.arange(half, dtype=jnp.float32) * 2.0 / vectors.shape[-1])
    angles = positions.astype(jnp.float32)[..., None] * freqs
    cosine = jnp.cos(angles)[..., None, :]
    sine = jnp.sin(angles)[..., None, :]
    values = vectors.astype(jnp.float32)
    first = values[..., :half]
    second = values[..., half:]
    return jnp.concatenate(
        [first * cosine - second * sine, second * cosine + first * sine], axis=-1
    ).astype(jnp.bfloat16)


def gather_rounds(x, axes, index, masks):
    count = 1 << len(masks)
    buf = x
    bits = []
    for mask in masks:
        low = mask & (-mask)
        bit = low if mask == low else mask - low
        perm = [(i, i ^ mask) for i in range(count)]
        recv = lax.ppermute(buf, axes, perm)
        mine = (index // bit) % 2
        buf = jnp.where(mine == 0, jnp.stack([buf, recv]), jnp.stack([recv, buf]))
        bits.append(bit)
    depth = len(bits)
    order = sorted(range(depth), key=lambda a: -bits[depth - 1 - a])
    buf = jnp.transpose(buf, tuple(order) + tuple(range(depth, buf.ndim)))
    return buf.reshape((count,) + x.shape)


def scatter_rounds(x, axes, index, wire=jnp.float32):
    count = x.shape[0]
    buf = x
    bit = 1
    while bit < count:
        pairs = buf.reshape((buf.shape[0] // 2, 2) + buf.shape[1:])
        mine = (index // bit) % 2
        keep = jnp.where(mine == 0, pairs[:, 0], pairs[:, 1])
        send = jnp.where(mine == 0, pairs[:, 1], pairs[:, 0])
        perm = [(i, i ^ bit) for i in range(count)]
        recv = lax.ppermute(send.astype(wire), axes, perm)
        buf = keep + recv.astype(keep.dtype)
        bit *= 2
    return buf[0]


def gather_masks(n_req, tp_count):
    masks = []
    for shift, size in ((tp_count.bit_length() - 1, n_req), (3, 4), (1, 4)):
        low = 1 << shift
        masks.append(low)
        if size == 4:
            masks.append(3 * low)
    masks.append(1)
    return masks


def per_device(
    step_inputs,
    qkv_weight,
    qkv_bias,
    out_weight,
    gate_weight,
    up_weight,
    down_weight,
    cache_keys,
    cache_values,
    lengths,
    parents,
    slot_request,
):
    steps, rows_dev, width = step_inputs.shape
    beams = parents.shape[2]
    requests = slot_request.shape[0]
    n_req = lax.axis_size("req")
    n_o = lax.axis_size("tpo")
    n_i = lax.axis_size("tpi")
    tp_count = n_o * n_i
    group_requests = requests // n_req
    group_rows = group_requests * beams
    owned, context, kv_width = cache_keys.shape
    head_dim = kv_width // KV_HEADS
    group = Q_HEADS // KV_HEADS
    attn_width = Q_HEADS * head_dim
    scale = head_dim ** (-0.5)
    assert owned * n_i == beams

    req_index = lax.axis_index("req")
    tp_index = lax.axis_index("tpo") * n_i + lax.axis_index("tpi")
    j = lax.axis_index("tpi")
    flat = req_index * tp_count + tp_index
    r = flat // n_i

    inverse = (
        jnp.zeros((requests,), jnp.int32)
        .at[slot_request]
        .set(jnp.arange(requests, dtype=jnp.int32))
    )

    flat_masks = gather_masks(n_req, tp_count)
    x_all = gather_rounds(
        jnp.swapaxes(step_inputs, 0, 1).reshape(rows_dev * steps, width), ALL, flat, flat_masks
    ).reshape(requests * beams, steps, width)
    full_out = lax.all_gather(out_weight, TP, axis=0, tiled=True)
    x_req = lax.dynamic_slice_in_dim(x_all, inverse[r] * beams, beams, 0)
    x_group = lax.dynamic_slice_in_dim(x_all, req_index * group_rows, group_rows, 0)

    normed = rms_normed(x_req)
    qkv = (
        jnp.dot(normed, qkv_weight, preferred_element_type=jnp.float32) + qkv_bias
    ).astype(jnp.bfloat16)

    par = parents[:, r, :]
    root = jnp.arange(beams, dtype=jnp.int32)
    roots = []
    for t in range(steps):
        root = root[par[t]]
        roots.append(root)
    roots = jnp.stack(roots, axis=1)
    len_r = lengths[r]
    positions = len_r[roots] + jnp.arange(steps, dtype=jnp.int32)[None, :]

    queries = rotate(qkv[..., :attn_width].reshape(beams, steps, Q_HEADS, head_dim), positions)
    new_keys = rotate(
        qkv[..., attn_width : attn_width + kv_width].reshape(beams, steps, KV_HEADS, head_dim),
        positions,
    )
    new_values = qkv[..., attn_width + kv_width :].reshape(beams, steps, KV_HEADS, head_dim)

    qg = queries.reshape(beams, steps, KV_HEADS, group, head_dim)
    score_parts = []
    for k in range(KV_HEADS):
        keys_k = cache_keys[:, :, k * head_dim : (k + 1) * head_dim]
        score_parts.append(
            jnp.einsum("btgd,cpd->cbtgp", qg[:, :, k], keys_k, preferred_element_type=jnp.float32)
        )
    scores = jnp.stack(score_parts, axis=3) * scale
    my_beams = j * owned + jnp.arange(owned, dtype=jnp.int32)
    limits = len_r[my_beams]
    live = (jnp.arange(context, dtype=jnp.int32)[None, :] < limits[:, None])[
        :, None, None, None, None, :
    ]
    scores = jnp.where(live, scores, masked_score)
    peak = jnp.max(scores, axis=-1)
    weights = jnp.where(live, jnp.exp(scores - peak[..., None]), 0.0)
    total = jnp.sum(weights, axis=-1)
    weights = weights.astype(jnp.bfloat16)
    output = jnp.stack(
        [
            jnp.einsum(
                "cbtgp,cpd->cbtgd",
                weights[:, :, :, k],
                cache_values[:, :, k * head_dim : (k + 1) * head_dim],
                preferred_element_type=jnp.float32,
            )
            for k in range(KV_HEADS)
        ],
        axis=3,
    )
    chosen = (roots[None, :, :] == my_beams[:, None, None])[..., None, None]
    peak = jnp.sum(jnp.where(chosen, peak, 0.0), axis=0)
    total = jnp.sum(jnp.where(chosen, total, 0.0), axis=0)
    output = jnp.sum(jnp.where(chosen[..., None], output, 0.0), axis=0)
    packed = jnp.concatenate([output, peak[..., None], total[..., None]], axis=-1)
    packed = packed.reshape(n_i, owned, steps, KV_HEADS, group, head_dim + 2)
    packed = scatter_rounds(packed, "tpi", j)
    part_output = packed[..., :head_dim]
    part_peak = packed[..., head_dim]
    part_total = packed[..., head_dim + 1]

    anc = []
    for t in range(steps):
        cur = jnp.arange(beams, dtype=jnp.int32)
        row = [None] * steps
        row[t] = cur
        for step in range(t, 0, -1):
            cur = par[step][cur]
            row[step - 1] = cur
        for u in range(t + 1, steps):
            row[u] = jnp.arange(beams, dtype=jnp.int32)
        anc.append(jnp.stack(row, axis=0))
    anc = jnp.stack(anc, axis=0)
    anc_mine = lax.dynamic_slice_in_dim(anc, j * owned, owned, 2)
    anc_mine = jnp.transpose(anc_mine, (2, 0, 1))
    u_index = jnp.broadcast_to(jnp.arange(steps, dtype=jnp.int32), anc_mine.shape)
    hist_keys = new_keys[anc_mine, u_index]
    hist_values = new_values[anc_mine, u_index]
    q_mine = lax.dynamic_slice_in_dim(qg, j * owned, owned, 0)
    recent_scores = jnp.einsum(
        "ctkgd,ctukd->ctkgu", q_mine, hist_keys, preferred_element_type=jnp.float32
    ) * scale
    causal = (
        jnp.arange(steps, dtype=jnp.int32)[None, :] <= jnp.arange(steps, dtype=jnp.int32)[:, None]
    )[None, :, None, None, :]
    recent_scores = jnp.where(causal, recent_scores, masked_score)
    top = jnp.maximum(part_peak, jnp.max(recent_scores, axis=-1))
    factor = jnp.exp(part_peak - top)
    recent_weights = jnp.where(causal, jnp.exp(recent_scores - top[..., None]), 0.0)
    denominator = part_total * factor + jnp.sum(recent_weights, axis=-1)
    numerator = part_output * factor[..., None] + jnp.einsum(
        "ctkgu,ctukd->ctkgd",
        recent_weights.astype(jnp.bfloat16),
        hist_values,
        preferred_element_type=jnp.float32,
    )
    attention = (
        (numerator / denominator[..., None]).reshape(owned, steps, attn_width).astype(jnp.bfloat16)
    )

    att_all = gather_rounds(attention, ALL, flat, flat_masks).reshape(
        requests * beams, steps, attn_width
    )
    my_requests = lax.dynamic_slice_in_dim(slot_request, req_index * group_requests, group_requests)
    att_group = att_all.reshape(requests, beams, steps, attn_width)[my_requests].reshape(
        group_rows, steps, attn_width
    )

    middle = x_group.astype(jnp.float32) + jnp.dot(
        att_group, full_out, preferred_element_type=jnp.float32
    )
    mixed_in = rms_normed(middle)
    gate = jnp.dot(mixed_in, gate_weight, preferred_element_type=jnp.float32)
    upward = jnp.dot(mixed_in, up_weight, preferred_element_type=jnp.float32)
    hidden = (jax.nn.silu(gate) * upward).astype(jnp.bfloat16)
    partial = jnp.dot(hidden, down_weight, preferred_element_type=jnp.float32)
    partial = scatter_rounds(
        partial.reshape(tp_count, rows_dev * steps, width), TP, tp_index, wire=jnp.bfloat16
    )
    lowered = partial.reshape(rows_dev, steps, width)
    middle_mine = lax.dynamic_slice_in_dim(middle, tp_index * rows_dev, rows_dev, 0)
    result = (middle_mine + lowered).astype(jnp.bfloat16)
    return jnp.swapaxes(result, 0, 1)


def solution(mesh):
    n_req = mesh.shape["req"]
    n_tp = mesh.shape["tp"]
    inner = 4
    devices = mesh.devices.reshape(n_req, n_tp // inner, inner)
    sub = Mesh(devices, ALL)
    rows = P(None, ALL, None)
    in_specs = (
        rows,
        P(),
        P(),
        P(TP, None),
        P(None, TP),
        P(None, TP),
        P(TP, None),
        P(ALL, None, None),
        P(ALL, None, None),
        P(),
        P(),
        P(),
    )
    return jax.shard_map(per_device, mesh=sub, in_specs=in_specs, out_specs=rows, check_vma=False)
```

```python
import jax
import jax.numpy as jnp
from jax import lax
from jax.sharding import Mesh
from jax.sharding import PartitionSpec as P

Q_HEADS = 12
KV_HEADS = 2

theta_base = 1000000.0
norm_eps = 1e-06
masked_score = -1e30

ALL = ("req", "tpo", "tpi")
TP = ("tpo", "tpi")


def rms_normed(values):
    values = values.astype(jnp.float32)
    factor = lax.rsqrt(jnp.mean(values * values, axis=-1, keepdims=True) + norm_eps)
    return (values * factor).astype(jnp.bfloat16)


def rotate(vectors, positions):
    half = vectors.shape[-1] // 2
    freqs = theta_base ** (-jnp.arange(half, dtype=jnp.float32) * 2.0 / vectors.shape[-1])
    angles = positions.astype(jnp.float32)[..., None] * freqs
    cosine = jnp.cos(angles)[..., None, :]
    sine = jnp.sin(angles)[..., None, :]
    values = vectors.astype(jnp.float32)
    first = values[..., :half]
    second = values[..., half:]
    return jnp.concatenate(
        [first * cosine - second * sine, second * cosine + first * sine], axis=-1
    ).astype(jnp.bfloat16)


def gather_rounds(x, axes, index, masks):
    count = 1 << len(masks)
    buf = x
    bits = []
    for mask in masks:
        low = mask & (-mask)
        bit = low if mask == low else mask - low
        perm = [(i, i ^ mask) for i in range(count)]
        recv = lax.ppermute(buf, axes, perm)
        mine = (index // bit) % 2
        buf = jnp.where(mine == 0, jnp.stack([buf, recv]), jnp.stack([recv, buf]))
        bits.append(bit)
    depth = len(bits)
    order = sorted(range(depth), key=lambda a: -bits[depth - 1 - a])
    buf = jnp.transpose(buf, tuple(order) + tuple(range(depth, buf.ndim)))
    return buf.reshape((count,) + x.shape)


def scatter_rounds(x, axes, index, wire=jnp.float32):
    count = x.shape[0]
    buf = x
    bit = 1
    while bit < count:
        pairs = buf.reshape((buf.shape[0] // 2, 2) + buf.shape[1:])
        mine = (index // bit) % 2
        keep = jnp.where(mine == 0, pairs[:, 0], pairs[:, 1])
        send = jnp.where(mine == 0, pairs[:, 1], pairs[:, 0])
        perm = [(i, i ^ bit) for i in range(count)]
        recv = lax.ppermute(send.astype(wire), axes, perm)
        buf = keep + recv.astype(keep.dtype)
        bit *= 2
    return buf[0]


def scatter_ring(x, axes, index, masks, wire):
    count = x.shape[0]
    depth = count.bit_length() - 1
    buf = x.reshape((2,) * depth + x.shape[1:])
    axis_bits = [1 << (depth - 1 - a) for a in range(depth)]
    for mask in masks:
        low = mask & (-mask)
        bit = low if mask == low else mask - low
        ax = axis_bits.index(bit)
        mine = (index // bit) % 2
        first = lax.index_in_dim(buf, 0, ax, keepdims=False)
        second = lax.index_in_dim(buf, 1, ax, keepdims=False)
        keep = jnp.where(mine == 0, first, second)
        send = jnp.where(mine == 0, second, first)
        perm = [(i, i ^ mask) for i in range(count)]
        recv = lax.ppermute(send.astype(wire), axes, perm)
        buf = keep + recv.astype(keep.dtype)
        axis_bits.pop(ax)
    return buf


def gather_masks(n_req, tp_count):
    masks = []
    for shift, size in ((tp_count.bit_length() - 1, n_req), (3, 4), (1, 4)):
        low = 1 << shift
        masks.append(low)
        if size == 4:
            masks.append(3 * low)
    masks.append(1)
    return masks


def per_device(
    step_inputs,
    qkv_weight,
    qkv_bias,
    out_weight,
    gate_weight,
    up_weight,
    down_weight,
    cache_keys,
    cache_values,
    lengths,
    parents,
    slot_request,
):
    steps, rows_dev, width = step_inputs.shape
    beams = parents.shape[2]
    requests = slot_request.shape[0]
    n_req = lax.axis_size("req")
    n_o = lax.axis_size("tpo")
    n_i = lax.axis_size("tpi")
    tp_count = n_o * n_i
    group_requests = requests // n_req
    group_rows = group_requests * beams
    owned, context, kv_width = cache_keys.shape
    head_dim = kv_width // KV_HEADS
    group = Q_HEADS // KV_HEADS
    attn_width = Q_HEADS * head_dim
    scale = head_dim ** (-0.5)
    assert owned * n_i == beams

    req_index = lax.axis_index("req")
    tp_index = lax.axis_index("tpo") * n_i + lax.axis_index("tpi")
    j = lax.axis_index("tpi")
    flat = req_index * tp_count + tp_index
    r = flat // n_i

    inverse = (
        jnp.zeros((requests,), jnp.int32)
        .at[slot_request]
        .set(jnp.arange(requests, dtype=jnp.int32))
    )

    flat_masks = gather_masks(n_req, tp_count)
    x_all = gather_rounds(
        jnp.swapaxes(step_inputs, 0, 1).reshape(rows_dev * steps, width), ALL, flat, flat_masks
    ).reshape(requests * beams, steps, width)
    full_out = lax.all_gather(out_weight, TP, axis=0, tiled=True)
    x_req = lax.dynamic_slice_in_dim(x_all, inverse[r] * beams, beams, 0)
    x_group = lax.dynamic_slice_in_dim(x_all, req_index * group_rows, group_rows, 0)

    normed = rms_normed(x_req)
    qkv = (
        jnp.dot(normed, qkv_weight, preferred_element_type=jnp.float32) + qkv_bias
    ).astype(jnp.bfloat16)

    par = parents[:, r, :]
    root = jnp.arange(beams, dtype=jnp.int32)
    roots = []
    for t in range(steps):
        root = root[par[t]]
        roots.append(root)
    roots = jnp.stack(roots, axis=1)
    len_r = lengths[r]
    positions = len_r[roots] + jnp.arange(steps, dtype=jnp.int32)[None, :]

    queries = rotate(qkv[..., :attn_width].reshape(beams, steps, Q_HEADS, head_dim), positions)
    new_keys = rotate(
        qkv[..., attn_width : attn_width + kv_width].reshape(beams, steps, KV_HEADS, head_dim),
        positions,
    )
    new_values = qkv[..., attn_width + kv_width :].reshape(beams, steps, KV_HEADS, head_dim)

    qg = queries.reshape(beams, steps, KV_HEADS, group, head_dim)
    score_parts = []
    for k in range(KV_HEADS):
        keys_k = cache_keys[:, :, k * head_dim : (k + 1) * head_dim]
        score_parts.append(
            jnp.einsum("btgd,cpd->cbtgp", qg[:, :, k], keys_k, preferred_element_type=jnp.float32)
        )
    scores = jnp.stack(score_parts, axis=3) * scale
    my_beams = j * owned + jnp.arange(owned, dtype=jnp.int32)
    limits = len_r[my_beams]
    live = (jnp.arange(context, dtype=jnp.int32)[None, :] < limits[:, None])[
        :, None, None, None, None, :
    ]
    scores = jnp.where(live, scores, masked_score)
    peak = jnp.max(scores, axis=-1)
    weights = jnp.where(live, jnp.exp(scores - peak[..., None]), 0.0)
    total = jnp.sum(weights, axis=-1)
    weights = weights.astype(jnp.bfloat16)
    output = jnp.stack(
        [
            jnp.einsum(
                "cbtgp,cpd->cbtgd",
                weights[:, :, :, k],
                cache_values[:, :, k * head_dim : (k + 1) * head_dim],
                preferred_element_type=jnp.float32,
            )
            for k in range(KV_HEADS)
        ],
        axis=3,
    )
    chosen = (roots[None, :, :] == my_beams[:, None, None])[..., None, None]
    peak = jnp.sum(jnp.where(chosen, peak, 0.0), axis=0)
    total = jnp.sum(jnp.where(chosen, total, 0.0), axis=0)
    output = jnp.sum(jnp.where(chosen[..., None], output, 0.0), axis=0)
    packed = jnp.concatenate([output, peak[..., None], total[..., None]], axis=-1)
    packed = packed.reshape(n_i, owned, steps, KV_HEADS, group, head_dim + 2)
    packed = scatter_rounds(packed, "tpi", j)
    part_output = packed[..., :head_dim]
    part_peak = packed[..., head_dim]
    part_total = packed[..., head_dim + 1]

    anc = []
    for t in range(steps):
        cur = jnp.arange(beams, dtype=jnp.int32)
        row = [None] * steps
        row[t] = cur
        for step in range(t, 0, -1):
            cur = par[step][cur]
            row[step - 1] = cur
        for u in range(t + 1, steps):
            row[u] = jnp.arange(beams, dtype=jnp.int32)
        anc.append(jnp.stack(row, axis=0))
    anc = jnp.stack(anc, axis=0)
    anc_mine = lax.dynamic_slice_in_dim(anc, j * owned, owned, 2)
    anc_mine = jnp.transpose(anc_mine, (2, 0, 1))
    u_index = jnp.broadcast_to(jnp.arange(steps, dtype=jnp.int32), anc_mine.shape)
    hist_keys = new_keys[anc_mine, u_index]
    hist_values = new_values[anc_mine, u_index]
    q_mine = lax.dynamic_slice_in_dim(qg, j * owned, owned, 0)
    recent_scores = jnp.einsum(
        "ctkgd,ctukd->ctkgu", q_mine, hist_keys, preferred_element_type=jnp.float32
    ) * scale
    causal = (
        jnp.arange(steps, dtype=jnp.int32)[None, :] <= jnp.arange(steps, dtype=jnp.int32)[:, None]
    )[None, :, None, None, :]
    recent_scores = jnp.where(causal, recent_scores, masked_score)
    top = jnp.maximum(part_peak, jnp.max(recent_scores, axis=-1))
    factor = jnp.exp(part_peak - top)
    recent_weights = jnp.where(causal, jnp.exp(recent_scores - top[..., None]), 0.0)
    denominator = part_total * factor + jnp.sum(recent_weights, axis=-1)
    numerator = part_output * factor[..., None] + jnp.einsum(
        "ctkgu,ctukd->ctkgd",
        recent_weights.astype(jnp.bfloat16),
        hist_values,
        preferred_element_type=jnp.float32,
    )
    attention = (
        (numerator / denominator[..., None]).reshape(owned, steps, attn_width).astype(jnp.bfloat16)
    )

    att_all = gather_rounds(attention, ALL, flat, flat_masks).reshape(
        requests * beams, steps, attn_width
    )
    my_requests = lax.dynamic_slice_in_dim(slot_request, req_index * group_requests, group_requests)
    att_group = att_all.reshape(requests, beams, steps, attn_width)[my_requests].reshape(
        group_rows, steps, attn_width
    )

    middle = x_group.astype(jnp.float32) + jnp.dot(
        att_group, full_out, preferred_element_type=jnp.float32
    )
    mixed_in = rms_normed(middle)
    gate = jnp.dot(mixed_in, gate_weight, preferred_element_type=jnp.float32)
    upward = jnp.dot(mixed_in, up_weight, preferred_element_type=jnp.float32)
    hidden = (jax.nn.silu(gate) * upward).astype(jnp.bfloat16)
    partial = jnp.dot(hidden, down_weight, preferred_element_type=jnp.float32)
    partial = scatter_ring(
        partial.reshape(tp_count, rows_dev * steps, width), TP, tp_index, [1, 6, 2, 24, 8], jnp.bfloat16
    )[None]
    lowered = partial.reshape(rows_dev, steps, width)
    middle_mine = lax.dynamic_slice_in_dim(middle, tp_index * rows_dev, rows_dev, 0)
    result = (middle_mine + lowered).astype(jnp.bfloat16)
    return jnp.swapaxes(result, 0, 1)


def solution(mesh):
    n_req = mesh.shape["req"]
    n_tp = mesh.shape["tp"]
    inner = 4
    devices = mesh.devices.reshape(n_req, n_tp // inner, inner)
    sub = Mesh(devices, ALL)
    rows = P(None, ALL, None)
    in_specs = (
        rows,
        P(),
        P(),
        P(TP, None),
        P(None, TP),
        P(None, TP),
        P(TP, None),
        P(ALL, None, None),
        P(ALL, None, None),
        P(),
        P(),
        P(),
    )
    return jax.shard_map(per_device, mesh=sub, in_specs=in_specs, out_specs=rows, check_vma=False)
```
